256 devices in a mesh: chan: 16 (over z, x_lo), stn: 16 (over x_hi, y, core).
Axes of the slice: x: 4 (x_hi: 2, x_lo: 2; x = x_hi * 2 + x_lo), y: 4, z: 8, core: 2. Of those that a mesh axis runs over, the one named last changes fastest.
Arguments:
- voltages: bfloat16 [128, 512, 4096], P('chan', 'stn'), may hold values from -6 to 6
- kernels: bfloat16 [128, 2, 8], P('chan'), may hold values from 0.049804688 to 0.5
- tile_lists: int32 [128, 16, 64, 128], P('chan', 'stn'), may hold values from 0 to 9216, as said below
- offset_u: int32 [128, 16, 64, 128], P('chan', 'stn'), may hold values from 0 to 24
- offset_v: int32 [128, 16, 64, 128], P('chan', 'stn'), may hold values from 0 to 24
- owner_map: int32 [128, 64], P('chan'), may hold values from 0 to 255
Outputs:
- grid_tiles: float32 [256, 2048], P(('chan', 'stn'))
The draws below stay inside these ranges and needn't reach their ends.
Inputs may be any that keep to these rules, and one draw needn't show every extreme that they name: `tile_lists`: each list holds its live baseline indices first and the value 9 * 32 * 32 (no baseline) in the remaining slots; in every channel and group one tile's list is full, and the others hold 32 to 128 live entries; no baseline appears twice in one channel and group while 64 * 128 <= 9216.
All inputs are finite; a program needn't handle non-finite values.
Results may differ from the reference program's by a relative error of at most 0.004.
Values may be sent and summed in bfloat16 or wider, within the bound.
A program may use at most 128 MiB of HBM per device.

```python
import math
import jax
import jax.numpy as jnp
from jax import lax

STN_GRP = 32
SAMPLES = 1024
TILE = 32
KW = 8
TILES_CH = 64
CAP = 128
STATIONS = 512
CHANNELS = 128
SHIFTS = 9
GRID_TILES = 256
N_STN = 16


def draw_tile_lists(key, part):
    total = SHIFTS * STN_GRP * STN_GRP

    def one_list_set(sub_key):
        key_perm, key_count, key_full = jax.random.split(sub_key, 3)
        order = jax.random.permutation(key_perm, total)
        counts = jax.random.randint(key_count, (TILES_CH,), CAP // 4, CAP + 1)
        full_tile = jax.random.randint(key_full, (), 0, TILES_CH)
        counts = jnp.where(jnp.arange(TILES_CH) == full_tile, CAP, counts)
        entry = jnp.arange(TILES_CH)[:, None] * CAP + jnp.arange(CAP)[None, :]
        chosen = order[entry % total]
        return jnp.where(jnp.arange(CAP)[None, :] < counts[:, None], chosen, total)
    keys = jax.random.split(jax.random.fold_in(key, 17), CHANNELS * N_STN)
    lists = jax.vmap(one_list_set)(keys)
    return lists.reshape(CHANNELS, N_STN, TILES_CH, CAP).astype(jnp.int32)


def with_ends(array, own_key, smallest, high):
    place = [jax.random.randint(jax.random.fold_in(own_key, axis), (), 0, length) for axis, length in enumerate(array.shape)]
    main_axis = array.shape.index(max(array.shape))
    neighbour = place[:main_axis] + [(place[main_axis] + 1) % array.shape[main_axis]] + place[main_axis + 1:]
    return array.at[tuple(place)].set(smallest).at[tuple(neighbour)].set(high)


def shard_levels(stream_key, extent, pieces, low, top_value):
    def one(axis_at, parts):
        draws = jax.random.uniform(jax.random.fold_in(jax.random.fold_in(stream_key, 6), axis_at), (parts,), jnp.float32, low / len(pieces), top_value / len(pieces))
        return jnp.repeat(jnp.exp(draws), extent[axis_at] // parts).reshape((-1,) + (1,) * (len(extent) - axis_at - 1))

    level = one(*pieces[0])
    for cut in pieces[1:]:
        level = level * one(*cut)
    return level


def scatter_about(own_key, extent, spread, most, pieces=(), kind=jnp.bfloat16):
    level = shard_levels(own_key, extent, pieces, -0.22, 0.18) if pieces else 1.0
    array = jax.random.normal(own_key, extent, jnp.float32) * spread * level
    return jnp.minimum(jnp.maximum(array, -most), most).astype(kind)


def setup_inputs(seed: int = 0) -> dict:
    splits = jax.random.split(jax.random.key(seed), 7)
    voltages = scatter_about(splits[0], (CHANNELS, STATIONS, 4 * SAMPLES), 1.0, 6.0, ((0, 16), (1, 16)))
    kernels = jnp.clip(jnp.exp(math.log(0.5) - 2.306499 * jax.random.uniform(splits[1], (CHANNELS, 2, KW), jnp.float32) ** shard_levels(splits[1], (CHANNELS, 2, KW), ((0, 16),), -0.2, 0.2)), 0.049804688, 0.5).astype(jnp.bfloat16)
    tile_lists = draw_tile_lists(jax.random.fold_in(splits[6], 71), 0)
    offset_u = with_ends(jax.random.randint(splits[3], (CHANNELS, N_STN, TILES_CH, CAP), 0, TILE - KW + 1), jax.random.fold_in(splits[3], 1), 0, TILE - KW).astype(jnp.int32)
    offset_v = with_ends(jax.random.randint(splits[4], (CHANNELS, N_STN, TILES_CH, CAP), 0, TILE - KW + 1), jax.random.fold_in(splits[4], 1), 0, TILE - KW).astype(jnp.int32)
    owner_map = with_ends(jax.random.randint(splits[5], (CHANNELS, TILES_CH), 0, GRID_TILES), jax.random.fold_in(splits[5], 1), 0, GRID_TILES - 1).astype(jnp.int32)
    return {"voltages": voltages, "kernels": kernels, "tile_lists": tile_lists, "offset_u": offset_u, "offset_v": offset_v, "owner_map": owner_map}


def rotate_parts(block):
    half_width = block.shape[-1] // 2
    return jnp.concatenate([-block[..., half_width:], block[..., :half_width]], axis=-1)

def kernel_rows(offsets, taps):
    cell_ids = jnp.arange(TILE, dtype=jnp.int32)
    distance = cell_ids[None, None, None, :] - offsets[..., None]
    result = jnp.zeros(distance.shape, jnp.float32)
    for tap in range(KW):
        result = result + jnp.where(distance == tap, taps[tap].astype(jnp.float32), jnp.float32(0.0))
    return result

def reference(voltages, kernels, tile_lists, offset_u, offset_v, owner_map):
    half_loop = N_STN // 2
    width = 4 * SAMPLES
    norm_scale = 1.0 / math.sqrt(width)
    group_ids = jnp.arange(N_STN, dtype=jnp.int32)[:, None, None, None, None]
    shift_ids = jnp.arange(SHIFTS, dtype=jnp.int32)[None, :, None, None, None]
    row_ids = jnp.arange(STN_GRP, dtype=jnp.int32)[None, None, :, None, None]
    col_ids = jnp.arange(STN_GRP, dtype=jnp.int32)[None, None, None, None, :]
    auto_mask = (shift_ids == 0) & (row_ids == col_ids)
    far_mask = (shift_ids == half_loop) & (group_ids >= half_loop)
    kept_mask = jnp.logical_not(auto_mask | far_mask)

    def one_channel(carry, inputs):
        volt, kern, entry_ids, off_u, off_v, owner = inputs
        groups = volt.astype(jnp.float32).reshape(N_STN, STN_GRP, width)
        blocks = []
        for step_count in range(half_loop + 1):
            other = jnp.roll(groups, -step_count, axis=0)
            paired = jnp.concatenate([other, rotate_parts(other)], axis=1)
            blocks.append(jnp.einsum('gik,gjk->gij', groups, paired, precision=lax.Precision.HIGHEST) * norm_scale)
        stacked = jnp.stack(blocks, axis=1).reshape(N_STN, SHIFTS, STN_GRP, 2, STN_GRP)
        vis = jnp.where(kept_mask, stacked, jnp.float32(0.0)).astype(jnp.bfloat16)
        flat_vis = jnp.transpose(vis, (0, 1, 2, 4, 3)).reshape(N_STN, SHIFTS * STN_GRP * STN_GRP, 2)
        flat_vis = jnp.concatenate([flat_vis, jnp.zeros((N_STN, 1, 2), jnp.bfloat16)], axis=1)
        picked = jax.vmap(lambda table, index: table[index])(flat_vis, entry_ids.reshape(N_STN, -1).astype(jnp.int32))
        picked = picked.reshape(N_STN, TILES_CH, CAP, 2)
        row_taps = kernel_rows(off_u, kern[0]).astype(jnp.bfloat16)
        col_taps = kernel_rows(off_v, kern[1]).astype(jnp.bfloat16)
        weighted = (picked.astype(jnp.float32)[..., :, None] * col_taps.astype(jnp.float32)[..., None, :]).astype(jnp.bfloat16)
        chan_tiles = jnp.einsum('gtku,gtkrv->truv', row_taps.astype(jnp.float32), weighted.astype(jnp.float32), precision=lax.Precision.HIGHEST)
        summed = jax.ops.segment_sum(chan_tiles.reshape(TILES_CH, -1), owner.astype(jnp.int32), num_segments=GRID_TILES)
        return (carry + summed, None)
    start = jnp.zeros((GRID_TILES, 2 * TILE * TILE), jnp.float32)
    result, unused = lax.scan(one_channel, start, (voltages, kernels, tile_lists, offset_u, offset_v, owner_map))
    return result
```

```python
import math

import jax
import jax.numpy as jnp
from jax import lax
from jax.experimental import pallas as pl
from jax.experimental.pallas import tpu as pltpu
from jax.sharding import PartitionSpec as P

MESH = pl.DeviceIdType.MESH
TILE = 32
GRP = 32
SAMPLES = 1024
TILES_CH = 64
CAP = 128
GRID_TILES = 256
TAB_ROWS = 40
F32 = jnp.float32
BF16 = jnp.bfloat16


def dot_nt(a, b):
    return lax.dot_general(a, b, (((1,), (1,)), ((), ())), preferred_element_type=F32)


def correlate_kernel(volt, lists, tab, lists_out, xs, neg, gram, got,
                     v_send, v_recv, l_send, l_recv, own_sem, e_send, e_recv):
    chan = lax.axis_index("chan")
    me = lax.axis_index("stn")
    chip = me // 2
    pol = lax.rem(me, 2)

    barrier = pltpu.get_barrier_semaphore()
    for j in range(1, 16):
        pl.semaphore_signal(barrier, 1, device_id=(chan, lax.rem(me + j, 16)), device_id_type=MESH)
    pl.semaphore_wait(barrier, 15)

    def volt_src(dest, half):
        return volt.at[dest // 2, :, pl.ds(pl.multiple_of(half * 2048 + lax.rem(dest, 2) * 1024, 1024), 1024)]

    def volt_dst(half):
        return xs.at[pl.ds(pl.multiple_of(me * GRP, GRP), GRP), pl.ds(half * 1024, 1024)]

    list_core = me // 8
    list_slot = lax.rem(me, 8)

    def list_copy(k):
        return pltpu.make_async_remote_copy(
            lists.at[k], lists_out.at[list_slot], l_send.at[k], l_recv.at[list_slot],
            device_id=(chan, 2 * k + list_core), device_id_type=MESH)

    def list_local(k):
        return pltpu.make_async_copy(lists.at[k], lists_out.at[list_slot], l_recv.at[list_slot])

    for k in range(8):
        @pl.when(2 * k + list_core != me)
        def _():
            list_copy(k).start()

        @pl.when(2 * k + list_core == me)
        def _():
            list_local(k).start()

    copies = []
    for half in range(2):
        for j in range(1, 16):
            dest = lax.rem(me + j, 16)
            copy = pltpu.make_async_remote_copy(
                volt_src(dest, half), volt_dst(half), v_send.at[half, j - 1], v_recv.at[half, j - 1],
                device_id=(chan, dest), device_id_type=MESH)
            copy.start()
            copies.append(copy)
    own = [pltpu.make_async_copy(volt_src(me, half), volt_dst(half), own_sem.at[half]) for half in range(2)]
    for copy in own:
        copy.start()
    for copy in own:
        copy.wait()
    for copy in copies:
        copy.wait()

    def products(block):
        row0 = pl.multiple_of(block * 256, 256)
        neg[:, :1024] = xs[pl.ds(row0, 256), 1024:]
        neg[:, 1024:] = -xs[pl.ds(row0, 256), :1024]
        for col in range(2):
            other = block if col == 0 else 1 - block
            right = xs[pl.ds(pl.multiple_of(other * 256, 256), 256), :]
            gram[block, 0, :, col * 256:(col + 1) * 256] = dot_nt(xs[pl.ds(row0, 256), :], right)
            gram[block, 1, :, col * 256:(col + 1) * 256] = dot_nt(neg[...], right)

    products(1 - pol)
    exchange = pltpu.make_async_remote_copy(
        gram.at[1 - pol], got, e_send, e_recv, device_id=(chan, chip * 2 + 1 - pol), device_id_type=MESH)
    exchange.start()
    products(pol)
    exchange.wait()

    lane = lax.broadcasted_iota(jnp.int32, (GRP, 256), 1)
    row = lax.broadcasted_iota(jnp.int32, (GRP, 256), 0)
    lane8 = lax.broadcasted_iota(jnp.int32, (8, 128), 1)
    for g in range(8):
        for part in range(2):
            rows = slice(g * GRP, (g + 1) * GRP)
            full = (gram[pol, part, rows, :] + got[part, rows, :]) * (1.0 / 64.0)
            if g:
                full = pltpu.roll(full, 512 - g * GRP, 1)
            near = jnp.where(lane == row, 0.0, full[:, :256])
            far = jnp.zeros((8, 128), F32)
            for m in range(4):
                piece = full[m * 8:(m + 1) * 8, 256:384]
                if m:
                    piece = pltpu.roll(piece, m * 32, 1)
                far = jnp.where(lane8 // 32 == m, piece, far)
            far = jnp.where(pol == 0, far, 0.0)
            far = jnp.concatenate([far, jnp.zeros((8, 128), F32)], axis=1)
            tab[g, part * TAB_ROWS:(part + 1) * TAB_ROWS, :] = jnp.concatenate([near, far], axis=0).astype(BF16)

    for k in range(8):
        @pl.when(2 * k + list_core != me)
        def _():
            list_copy(k).wait_send()
    for slot in range(8):
        pltpu.make_async_copy(lists.at[0], lists_out.at[slot], l_recv.at[slot]).wait()


def correlate(voltages, lists):
    return pl.pallas_call(
        correlate_kernel,
        out_shape=(
            jax.ShapeDtypeStruct((8, 2 * TAB_ROWS, 256), BF16),
            jax.ShapeDtypeStruct((8, 3, TILES_CH, CAP), jnp.int16),
        ),
        in_specs=[pl.BlockSpec(memory_space=pl.ANY)] * 2,
        out_specs=(pl.BlockSpec(memory_space=pltpu.VMEM), pl.BlockSpec(memory_space=pltpu.VMEM)),
        scratch_shapes=[
            pltpu.VMEM((512, 2048), BF16),
            pltpu.VMEM((256, 2048), BF16),
            pltpu.VMEM((2, 2, 256, 512), F32),
            pltpu.VMEM((2, 256, 512), F32),
            pltpu.SemaphoreType.DMA((2, 15)),
            pltpu.SemaphoreType.DMA((2, 15)),
            pltpu.SemaphoreType.DMA((8,)),
            pltpu.SemaphoreType.DMA((8,)),
            pltpu.SemaphoreType.DMA((2,)),
            pltpu.SemaphoreType.DMA,
            pltpu.SemaphoreType.DMA,
        ],
        compiler_params=pltpu.CompilerParams(collective_id=0, has_side_effects=True),
        name="correlate",
    )(voltages, lists)


def split_dot(left, right, split_left):
    value = left if split_left else right
    high = value.astype(BF16)
    low = (value - high.astype(F32)).astype(BF16)
    if split_left:
        return (jnp.dot(high, right, preferred_element_type=F32)
                + jnp.dot(low, right, preferred_element_type=F32))
    return (jnp.dot(left, high, preferred_element_type=F32)
            + jnp.dot(left, low, preferred_element_type=F32))


def grid_kernel(kern, owner, tab, lists, grid, his, rows, offs_u, offs_v):
    for g in range(8):
        entry = lists[g, 0].astype(jnp.int32)
        shift = entry >> 10
        i = (entry >> 5) & 31
        j = entry & 31
        far = shift == 8
        his[g] = jnp.where(far, (i >> 3) * 32 + j, (shift & 7) * 32 + j)
        rows[g] = jnp.where(shift > 8, -1, jnp.where(far, 32 + (i & 7), i))
        offs_u[g] = lists[g, 1].astype(jnp.int32)
        offs_v[g] = lists[g, 2].astype(jnp.int32)
    grid[...] = jnp.zeros_like(grid)

    chip = lax.axis_index("stn") // 2
    dist = lax.broadcasted_iota(jnp.int32, (32, 128), 1) % 32 - lax.broadcasted_iota(jnp.int32, (32, 128), 0)
    taps_v = jnp.zeros((32, 128), F32)
    for tap in range(8):
        taps_v = jnp.where(dist == tap, kern[chip, 1, tap], taps_v)
    taps_v = taps_v.astype(BF16)
    ro = lax.broadcasted_iota(jnp.int32, (128, 128), 0)
    co = lax.broadcasted_iota(jnp.int32, (128, 128), 1)
    u = (ro % 8) * 4 + (ro % 64) // 16
    same = (ro // 64 == co // 64) & ((ro // 8) % 2 == (co // 32) % 2)
    dist = jnp.where(same, u - co % 32, -1)
    taps_u = jnp.zeros((128, 128), F32)
    for tap in range(8):
        taps_u = jnp.where(dist == tap, kern[chip, 0, tap], taps_u)
    taps_u = taps_u.astype(BF16)

    hot_ids = lax.broadcasted_iota(jnp.int32, (256, 128), 0)
    row_ids = lax.broadcasted_iota(jnp.int32, (TAB_ROWS, 128), 0)
    cell_ids = lax.broadcasted_iota(jnp.int32, (TILE, 128), 0)
    lane_grp = lax.broadcasted_iota(jnp.int32, (16, 128), 1) // 32

    def pair(tp, carry):
        sums = [None, None]
        for gp in range(4):
            left = [[], []]
            right = [[], []]
            for g in (2 * gp, 2 * gp + 1):
                hot = []
                for a in range(2):
                    hi = his[g, pl.ds(2 * tp + a, 1), :]
                    hot.append(jnp.where(hot_ids == hi, 1.0, 0.0).astype(BF16))
                found = jnp.dot(tab[g], jnp.concatenate(hot, axis=1), preferred_element_type=F32)
                for a in range(2):
                    lanes = slice(a * 128, (a + 1) * 128)
                    at_row = row_ids == rows[g, pl.ds(2 * tp + a, 1), :]
                    at_u = cell_ids == offs_u[g, pl.ds(2 * tp + a, 1), :]
                    at_v = cell_ids == offs_v[g, pl.ds(2 * tp + a, 1), :]
                    both = []
                    for part in range(2):
                        block = found[part * TAB_ROWS:(part + 1) * TAB_ROWS, lanes]
                        value = jnp.sum(jnp.where(at_row, block, 0.0), axis=0, keepdims=True)
                        both.append(jnp.where(at_u, value, 0.0))
                    left[a].append(jnp.concatenate(both, axis=0).astype(BF16))
                    right[a].append(jnp.where(at_v, 1.0, 0.0).astype(BF16))
            for a in range(2):
                term = dot_nt(jnp.concatenate(left[a], axis=1), jnp.concatenate(right[a], axis=1))
                sums[a] = term if sums[a] is None else sums[a] + term
        spread = split_dot(jnp.concatenate(sums, axis=0), taps_v, True)
        cells = split_dot(taps_u, spread, False)
        for a in range(2):
            tile = cells[a * 64:a * 64 + 16]
            for ul in range(1, 4):
                tile = jnp.where(lane_grp == ul, cells[a * 64 + ul * 16:a * 64 + ul * 16 + 16], tile)
            where = owner[chip, 2 * tp + a]
            grid[where] = grid[where] + tile
        return carry

    lax.fori_loop(0, TILES_CH // 2, pair, 0)


def grid_local(kern, owner, tab, lists):
    return pl.pallas_call(
        grid_kernel,
        out_shape=jax.ShapeDtypeStruct((GRID_TILES, 16, 128), F32),
        in_specs=[pl.BlockSpec(memory_space=pltpu.SMEM)] * 2 + [pl.BlockSpec(memory_space=pltpu.VMEM)] * 2,
        out_specs=pl.BlockSpec(memory_space=pltpu.VMEM),
        scratch_shapes=[pltpu.VMEM((8, TILES_CH, CAP), jnp.int32)] * 4,
        name="grid_local",
    )(kern, owner, tab, lists)


def reduce_kernel(part, out, got_c, send_a, send_b, got_a, got_b, sum_a, sum_b, got_a2, got_b2, sum_z, got_z,
                  sem_c, s_a, r_a, s_b, r_b, s_a2, r_a2, s_b2, r_b2, s_z, r_z):
    chan = lax.axis_index("chan")
    stn = lax.axis_index("stn")
    z, xlo = chan // 2, lax.rem(chan, 2)
    xhi, y, core = stn // 8, lax.rem(stn // 2, 4), lax.rem(stn, 2)
    x = xhi * 2 + xlo

    def device(x_, y_, z_, core_):
        return (z_ * 2 + lax.rem(x_, 2), (x_ // 2) * 8 + y_ * 2 + core_)

    def slot_x(x_):
        return lax.rem(x_, 2) * 2 + x_ // 2

    def peer_x(d):
        return lax.rem(x + d, 4)

    def peer_y(d):
        return lax.rem(y + d, 4)

    def peer_z(d):
        return lax.rem(z + d, 8)

    peers = [device(x, y, z, 1 - core)]
    peers += [device(peer_x(d), y, z, core) for d in range(1, 4)]
    peers += [device(x, peer_y(d), z, core) for d in range(1, 4)]
    peers += [device(x, y, peer_z(d), core) for d in range(1, 8)]
    barrier = pltpu.get_barrier_semaphore()
    for peer in peers:
        pl.semaphore_signal(barrier, 1, device_id=peer, device_id_type=MESH)
    pl.semaphore_wait(barrier, len(peers))

    def send(src, dst, ss, rs, peer):
        copy = pltpu.make_async_remote_copy(src, dst, ss, rs, device_id=peer, device_id_type=MESH)
        copy.start()
        return copy

    send(part.at[:, 1 - core], got_c, sem_c.at[0], sem_c.at[1], peers[0]).wait()

    def fold(n, carry):
        zq, xs = n // 4, lax.rem(n, 4)
        for yy in range(4):
            m = zq * 16 + xs * 4 + yy
            send_a[yy, n] = (part[m, core] + got_c[m]).astype(BF16)
            send_b[xs, zq * 4 + yy] = (part[64 + m, core] + got_c[64 + m]).astype(BF16)
        return carry

    lax.fori_loop(0, 16, fold, 0)
    first = []
    for d in range(1, 4):
        first.append(send(send_a.at[peer_y(d)], got_a.at[d - 1], s_a.at[d - 1], r_a.at[d - 1],
                          device(x, peer_y(d), z, core)))
        first.append(send(send_b.at[slot_x(peer_x(d))], got_b.at[d - 1], s_b.at[d - 1], r_b.at[d - 1],
                          device(peer_x(d), y, z, core)))
    for copy in first:
        copy.wait()

    def total_a(n, carry):
        m = n * 4 + y
        value = part[m, core] + got_c[m]
        for d in range(3):
            value = value + got_a[d, n].astype(F32)
        sum_a[lax.rem(n, 4), n // 4] = value
        zq, yy = n // 4, lax.rem(n, 4)
        m = 64 + zq * 16 + slot_x(x) * 4 + yy
        value = part[m, core] + got_c[m]
        for d in range(3):
            value = value + got_b[d, n].astype(F32)
        sum_b[yy, zq] = value
        return carry

    lax.fori_loop(0, 16, total_a, 0)
    second = []
    for d in range(1, 4):
        second.append(send(sum_a.at[slot_x(peer_x(d))], got_a2.at[d - 1], s_a2.at[d - 1], r_a2.at[d - 1],
                           device(peer_x(d), y, z, core)))
        second.append(send(sum_b.at[peer_y(d)], got_b2.at[d - 1], s_b2.at[d - 1], r_b2.at[d - 1],
                           device(x, peer_y(d), z, core)))
    for copy in second:
        copy.wait()
    sum_z[0:4] = sum_a[slot_x(x)] + got_a2[0] + got_a2[1] + got_a2[2]
    sum_z[4:8] = sum_b[y] + got_b2[0] + got_b2[1] + got_b2[2]
    third = []
    for d in range(1, 8):
        third.append(send(sum_z.at[peer_z(d)], got_z.at[d - 1], s_z.at[d - 1], r_z.at[d - 1],
                          device(x, y, peer_z(d), core)))
    for copy in third:
        copy.wait()
    value = sum_z[z]
    for d in range(7):
        value = value + got_z[d]
    out[...] = value


def reduce_grid(part):
    dma = pltpu.SemaphoreType.DMA
    return pl.pallas_call(
        reduce_kernel,
        out_shape=jax.ShapeDtypeStruct((16, 128), F32),
        in_specs=[pl.BlockSpec(memory_space=pltpu.VMEM)],
        out_specs=pl.BlockSpec(memory_space=pltpu.VMEM),
        scratch_shapes=[
            pltpu.VMEM((128, 16, 128), F32),
            pltpu.VMEM((4, 16, 16, 128), BF16),
            pltpu.VMEM((4, 16, 16, 128), BF16),
            pltpu.VMEM((3, 16, 16, 128), BF16),
            pltpu.VMEM((3, 16, 16, 128), BF16),
            pltpu.VMEM((4, 4, 16, 128), F32),
            pltpu.VMEM((4, 4, 16, 128), F32),
            pltpu.VMEM((3, 4, 16, 128), F32),
            pltpu.VMEM((3, 4, 16, 128), F32),
            pltpu.VMEM((8, 16, 128), F32),
            pltpu.VMEM((7, 16, 128), F32),
            dma((2,)),
            dma((3,)), dma((3,)), dma((3,)), dma((3,)),
            dma((3,)), dma((3,)), dma((3,)), dma((3,)),
            dma((7,)), dma((7,)),
        ],
        compiler_params=pltpu.CompilerParams(collective_id=1, has_side_effects=True),
        name="reduce_grid",
    )(part.reshape(128, 2, 16, 128))


def on_device(voltages, kernels, tile_lists, offset_u, offset_v, owner_map):
    lists = jnp.stack([tile_lists[:, 0], offset_u[:, 0], offset_v[:, 0]], axis=1).astype(jnp.int16)
    tab, lists_here = correlate(voltages, lists)
    part = grid_local(kernels.astype(F32), owner_map, tab, lists_here)
    return reduce_grid(part).reshape(1, -1)


def solution(mesh):
    placed = (
        P("chan", "stn", None),
        P("chan", None, None),
        P("chan", "stn", None, None),
        P("chan", "stn", None, None),
        P("chan", "stn", None, None),
        P("chan", None),
    )
    return jax.shard_map(
        on_device, mesh=mesh, in_specs=placed, out_specs=P(("chan", "stn"), None), check_vma=False
    )
```

```python
import math

import jax
import jax.numpy as jnp
from jax import lax
from jax.experimental import pallas as pl
from jax.experimental.pallas import tpu as pltpu
from jax.sharding import PartitionSpec as P

MESH = pl.DeviceIdType.MESH
TILE = 32
GRP = 32
SAMPLES = 1024
TILES_CH = 64
CAP = 128
GRID_TILES = 256
TAB_ROWS = 80
N_CHIPS = 8
F32 = jnp.float32
BF16 = jnp.bfloat16


def dot_nt(a, b):
    return lax.dot_general(a, b, (((1,), (1,)), ((), ())), preferred_element_type=F32)


def chan_kernel(volt, entries, off_u_in, off_v_in, kern, owner, out,
                xs, neg, gram, got, raw, packed, lists, tab, his, rows, offs_u, offs_v, buf0, buf1, sums,
                mine, theirs, dense, send_a, send_b, got_a, got_b, sum_a, sum_b, got_a2, got_b2, sum_z, got_z,
                raw_sem, v_send, v_recv, l_send, l_recv, own_sem, e_sem, t_send, t_recv,
                s_a, r_a, s_b, r_b, s_a2, r_a2, s_b2, r_b2, s_z, r_z):
    chan = lax.axis_index("chan")
    me = lax.axis_index("stn")
    chip = me // 2
    core = lax.rem(me, 2)
    z, xlo = chan // 2, lax.rem(chan, 2)
    xhi, y = me // 8, lax.rem(chip, 4)
    x = xhi * 2 + xlo

    def device(x_, y_, z_):
        return (z_ * 2 + lax.rem(x_, 2), (x_ // 2) * 8 + y_ * 2 + core)

    def slot_x(x_):
        return lax.rem(x_, 2) * 2 + x_ // 2

    def peer_x(d):
        return lax.rem(x + d, 4)

    def peer_y(d):
        return lax.rem(y + d, 4)

    def peer_z(d):
        return lax.rem(z + d, 8)

    partner = (chan, 2 * chip + 1 - core)
    peers = [(chan, lax.rem(me + j, 16)) for j in range(1, 16)]
    peers += [device(peer_x(d), y, z) for d in (1, 3)]
    peers += [device(x, y, peer_z(d)) for d in range(1, 8)]
    barrier = pltpu.get_barrier_semaphore()
    for peer in peers:
        pl.semaphore_signal(barrier, 1, device_id=peer, device_id_type=MESH)

    loads = [pltpu.make_async_copy(ref.at[:, 0], raw.at[n], raw_sem.at[n])
             for n, ref in enumerate((entries, off_u_in, off_v_in))]
    for copy in loads:
        copy.start()
    for copy in loads:
        copy.wait()

    def narrow(k, carry):
        for n in range(3):
            packed[k, n] = raw[n, k].astype(jnp.int16)
        return carry

    lax.fori_loop(0, N_CHIPS, narrow, 0)
    pl.semaphore_wait(barrier, len(peers))

    def send(src, dst, ss, rs, peer):
        copy = pltpu.make_async_remote_copy(src, dst, ss, rs, device_id=peer, device_id_type=MESH)
        copy.start()
        return copy

    list_core = me // 8
    list_slot = lax.rem(me, 8)

    def list_copy(k):
        return pltpu.make_async_remote_copy(
            packed.at[k], lists.at[list_slot], l_send.at[k], l_recv.at[list_slot],
            device_id=(chan, 2 * k + list_core), device_id_type=MESH)

    for k in range(N_CHIPS):
        @pl.when(2 * k + list_core != me)
        def _():
            list_copy(k).start()

        @pl.when(2 * k + list_core == me)
        def _():
            pltpu.make_async_copy(packed.at[k], lists.at[list_slot], l_recv.at[list_slot]).start()

    def volt_src(dest, half):
        return volt.at[dest // 2, :, pl.ds(pl.multiple_of(half * 2048 + lax.rem(dest, 2) * 1024, 1024), 1024)]

    def volt_dst(half):
        return xs.at[pl.ds(pl.multiple_of(me * GRP, GRP), GRP), pl.ds(half * 1024, 1024)]

    copies = []
    for half in range(2):
        for j in range(1, 16):
            dest = lax.rem(me + j, 16)
            copies.append(send(volt_src(dest, half), volt_dst(half), v_send.at[half, j - 1],
                               v_recv.at[half, j - 1], (chan, dest)))
    own = [pltpu.make_async_copy(volt_src(me, half), volt_dst(half), own_sem.at[half]) for half in range(2)]
    for copy in own:
        copy.start()

    for slot in range(8):
        pltpu.make_async_copy(packed.at[0], lists.at[slot], l_recv.at[slot]).wait()

    def prepare(g, carry):
        entry = lists[g, 0].astype(jnp.int32)
        shift = entry >> 10
        i = (entry >> 5) & 31
        j = entry & 31
        far = shift == 8
        his[g] = jnp.where(far, (i >> 3) * 32 + j, (shift & 7) * 32 + j)
        rows[g] = jnp.where(shift > 8, -1, jnp.where(far, 32 + (i & 7), i))
        offs_u[g] = lists[g, 1].astype(jnp.int32)
        offs_v[g] = lists[g, 2].astype(jnp.int32)
        return carry

    lax.fori_loop(0, 8, prepare, 0)
    iota = lambda shape, axis: lax.broadcasted_iota(jnp.int32, shape, axis)
    taps = kern[chip].astype(F32)
    dist = iota((64, 128), 1) % 32 - iota((64, 128), 0) % 32
    taps_v = jnp.zeros((64, 128), F32)
    for tap in range(8):
        taps_v = jnp.where(dist == tap, taps[1:2, tap:tap + 1], taps_v)
    taps_v = taps_v.astype(BF16)
    ro, co = iota((128, 128), 0), iota((128, 128), 1)
    u = (ro % 8) * 4 + (ro % 64) // 16
    same = (ro // 64 == co // 64) & ((ro // 8) % 2 == (co // 32) % 2)
    dist = jnp.where(same, u - co % 32, -1)
    taps_u = jnp.zeros((128, 128), F32)
    for tap in range(8):
        taps_u = jnp.where(dist == tap, taps[0:1, tap:tap + 1], taps_u)
    taps_u = taps_u.astype(BF16)
    taps_u = jnp.concatenate([taps_u, taps_u], axis=1)
    low = ro % 64
    outer, inner, zq = low // 16, (low // 4) % 4, low % 4
    ys = jnp.where(ro < 64, outer, inner)
    xslot = jnp.where(ro < 64, inner, outer)
    cell = (zq + 4 * (ro // 64)) * 32 + xslot * 8 + ys * 2 + core
    owners = owner[pl.ds(chip, 1), :]
    owners = jnp.concatenate([owners, owners], axis=1)
    owner_hot = jnp.where(cell == owners, 1.0, 0.0).astype(BF16)
    ro, co = iota((64, 48), 0), iota((64, 48), 1)
    spread_ones = jnp.where(jnp.where(co < 32, co // 16, (co - 32) // 8) == ro // 32, 1.0, 0.0).astype(BF16)

    for copy in own:
        copy.wait()
    for copy in copies:
        copy.wait()

    def products(block):
        row0 = pl.multiple_of(block * 256, 256)
        neg[:, :1024] = xs[pl.ds(row0, 256), 1024:]
        neg[:, 1024:] = -xs[pl.ds(row0, 256), :1024]
        for col in range(2):
            other = block if col == 0 else 1 - block
            right = xs[pl.ds(pl.multiple_of(other * 256, 256), 256), :]
            gram[block, 0, :, col * 256:(col + 1) * 256] = dot_nt(xs[pl.ds(row0, 256), :], right)
            gram[block, 1, :, col * 256:(col + 1) * 256] = dot_nt(neg[...], right)

    products(1 - core)
    exchange = send(gram.at[1 - core], got, e_sem.at[0], e_sem.at[1], partner)
    products(core)
    exchange.wait()

    lane, row = iota((GRP, 256), 1), iota((GRP, 256), 0)
    lane_grp8 = iota((8, 128), 1) // 32
    for g in range(8):
        fars = []
        for part in range(2):
            block = slice(g * GRP, (g + 1) * GRP)
            full = (gram[core, part, block, :] + got[part, block, :]) * (1.0 / 64.0)
            if g:
                full = pltpu.roll(full, 512 - g * GRP, 1)
            near = jnp.where(lane == row, 0.0, full[:, :256])
            tab[g, part * GRP:(part + 1) * GRP, :] = near.astype(BF16)
            far = jnp.zeros((8, 128), F32)
            for m in range(4):
                piece = full[m * 8:(m + 1) * 8, 256:384]
                if m:
                    piece = pltpu.roll(piece, m * 32, 1)
                far = jnp.where(lane_grp8 == m, piece, far)
            fars.append(jnp.where(core == 0, far, 0.0))
        far = jnp.concatenate(fars, axis=0)
        tab[g, 64:80, :] = jnp.concatenate([far, jnp.zeros((16, 128), F32)], axis=1).astype(BF16)

    ids16 = iota((16, 128), 0).astype(jnp.int16)
    hot_ids = [(iota((16, 128), 0) + 16 * n).astype(jnp.int16) for n in range(16)]
    far_ids = (iota((16, 128), 0) % 8 + 32).astype(jnp.int16)
    one, zero = jnp.ones((), BF16), jnp.zeros((), BF16)

    def line(ref, g, t):
        return jnp.broadcast_to(ref[g, pl.ds(t, 1), :], (16, 128)).astype(jnp.int16)

    def fetch(tp, buf, g):
        hot = []
        for a in range(2):
            hi = line(his, g, 2 * tp + a)
            hot.append(jnp.concatenate([jnp.where(ids == hi, one, zero) for ids in hot_ids], axis=0))
        buf[g] = jnp.dot(tab[g], jnp.concatenate(hot, axis=1), preferred_element_type=F32).astype(BF16)

    def place(tp, buf, g, left, right):
        picked = []
        for a in range(2):
            r = line(rows, g, 2 * tp + a)
            near, mid, far = ids16 == r, hot_ids[1] == r, far_ids == r
            lanes = slice(a * 128, (a + 1) * 128)
            tiles = [buf[g, n * 16:(n + 1) * 16, lanes] for n in range(5)]
            re = jnp.where(near, tiles[0], jnp.where(mid, tiles[1], zero))
            im = jnp.where(near, tiles[2], jnp.where(mid, tiles[3], zero))
            picked.append(jnp.concatenate([re, im, jnp.where(far, tiles[4], zero)], axis=0))
        wide = jnp.dot(spread_ones, jnp.concatenate(picked, axis=1), preferred_element_type=F32).astype(BF16)
        for a in range(2):
            lanes = slice(a * 128, (a + 1) * 128)
            at_u = line(offs_u, g, 2 * tp + a)
            at_v = line(offs_v, g, 2 * tp + a)
            masks = [ids16 == at_u, hot_ids[1] == at_u]
            left[a].append(jnp.concatenate(
                [jnp.where(masks[n % 2], wide[n * 16:(n + 1) * 16, lanes], zero) for n in range(4)], axis=0))
            right[a].append(jnp.concatenate(
                [jnp.where(ids == at_v, one, zero) for ids in (ids16, hot_ids[1])], axis=0))

    def stage(tp_next, buf_next, tp, buf):
        totals = [None, None]
        for gp in range(4):
            left, right = [[], []], [[], []]
            for g in (2 * gp, 2 * gp + 1):
                fetch(tp_next, buf_next, g)
                place(tp, buf, g, left, right)
            for a in range(2):
                twice = jnp.concatenate(right[a], axis=1)
                term = dot_nt(jnp.concatenate(left[a], axis=1), jnp.concatenate([twice, twice], axis=0))
                totals[a] = term if totals[a] is None else totals[a] + term
        for a in range(2):
            sums[2 * tp + a] = totals[a]

    for g in range(8):
        fetch(0, buf0, g)

    def pair(i, carry):
        stage(2 * i + 1, buf1, 2 * i, buf0)
        stage(lax.rem(2 * i + 2, TILES_CH // 2), buf0, 2 * i + 1, buf1)
        return carry

    lax.fori_loop(0, TILES_CH // 4, pair, 0)

    first_lanes = iota((128, 64), 1) < 32
    lane_grp = iota((16, 128), 1) // 32

    def tile_copy(step):
        part = pl.ds(pl.multiple_of(step * 8, 8), 8)
        return pltpu.make_async_remote_copy(mine.at[:, part], theirs.at[:, part], t_send.at[step], t_recv.at[step],
                                            device_id=partner, device_id_type=MESH)

    def finish(step, carry):
        for b in range(4):
            t = step * 8 + b * 2
            value = sums[pl.ds(t, 2)].reshape(128, 64)
            high = value.astype(BF16).astype(F32)
            mixed = jnp.where(first_lanes, high, value - high).astype(BF16)
            spread = jnp.dot(mixed, taps_v, preferred_element_type=F32)
            high = spread.astype(BF16)
            low_part = (spread - high.astype(F32)).astype(BF16)
            cells = jnp.dot(taps_u, jnp.concatenate([high, low_part], axis=0), preferred_element_type=F32)
            for a in range(2):
                tile = cells[a * 64:a * 64 + 16]
                for ul in range(1, 4):
                    tile = jnp.where(lane_grp == ul, cells[a * 64 + ul * 16:a * 64 + ul * 16 + 16], tile)
                mine.reshape(16 * TILES_CH, 128)[pl.ds(t + a, 16, stride=TILES_CH), :] = tile
        tile_copy(step).start()
        return carry

    lax.fori_loop(0, TILES_CH // 8, finish, 0)
    for step in range(TILES_CH // 8):
        tile_copy(step).wait()

    for a in range(16):
        value = mine[a] + theirs[a]
        high = value.astype(BF16)
        low_part = (value - high.astype(F32)).astype(BF16)
        cells = jnp.dot(owner_hot, jnp.concatenate([high, low_part], axis=0), preferred_element_type=F32)
        dense[a] = cells
        for n in range(4):
            send_a[n, a] = cells[n * 16:(n + 1) * 16].astype(BF16)
            send_b[n, a] = cells[64 + n * 16:64 + (n + 1) * 16].astype(BF16)

    first = []
    for d in (2, 1, 3):
        first.append(send(send_a.at[peer_y(d)], got_a.at[d - 1], s_a.at[d - 1], r_a.at[d - 1],
                          device(x, peer_y(d), z)))
        first.append(send(send_b.at[slot_x(peer_x(d))], got_b.at[d - 1], s_b.at[d - 1], r_b.at[d - 1],
                          device(peer_x(d), y, z)))
    for copy in first:
        copy.wait()
    at_a = pl.ds(pl.multiple_of(y * 16, 16), 16)
    at_b = pl.ds(pl.multiple_of(64 + slot_x(x) * 16, 16), 16)
    for a in range(16):
        value = dense[a, at_a, :]
        for d in range(3):
            value = value + got_a[d, a].astype(F32)
        sum_a.reshape(256, 128)[pl.ds(a, 16, stride=16), :] = value
        value = dense[a, at_b, :]
        for d in range(3):
            value = value + got_b[d, a].astype(F32)
        sum_b.reshape(256, 128)[pl.ds(a, 16, stride=16), :] = value

    def four(slot):
        return pl.ds(pl.multiple_of(slot * 4, 4), 4)

    second = []
    for d in (2, 1, 3):
        second.append(send(sum_a.at[four(slot_x(peer_x(d)))], got_a2.at[d - 1], s_a2.at[d - 1], r_a2.at[d - 1],
                           device(peer_x(d), y, z)))
        second.append(send(sum_b.at[four(peer_y(d))], got_b2.at[d - 1], s_b2.at[d - 1], r_b2.at[d - 1],
                           device(x, peer_y(d), z)))
    for copy in second:
        copy.wait()
    sum_z[0:4] = sum_a[four(slot_x(x))] + got_a2[0] + got_a2[1] + got_a2[2]
    sum_z[4:8] = sum_b[four(y)] + got_b2[0] + got_b2[1] + got_b2[2]
    third = []
    for d in (4, 3, 5, 2, 6, 1, 7):
        third.append(send(sum_z.at[peer_z(d)], got_z.at[d - 1], s_z.at[d - 1], r_z.at[d - 1],
                          device(x, y, peer_z(d))))
    for k in range(N_CHIPS):
        @pl.when(2 * k + list_core != me)
        def _():
            list_copy(k).wait_send()
    for copy in third:
        copy.wait()
    value = sum_z[z]
    for d in range(7):
        value = value + got_z[d]
    for n in range(16):
        out[:, n * 128:(n + 1) * 128] = value[n:n + 1]


def on_device(voltages, kernels, tile_lists, offset_u, offset_v, owner_map):
    dma = pltpu.SemaphoreType.DMA
    anywhere, vmem = pl.BlockSpec(memory_space=pl.ANY), pl.BlockSpec(memory_space=pltpu.VMEM)
    lists_shape = (8, 3, TILES_CH, CAP)
    return pl.pallas_call(
        chan_kernel,
        out_shape=jax.ShapeDtypeStruct((1, 2048), F32),
        in_specs=[anywhere] * 4 + [vmem] * 2,
        out_specs=vmem,
        scratch_shapes=[
            pltpu.VMEM((512, 2048), BF16),
            pltpu.VMEM((256, 2048), BF16),
            pltpu.VMEM((2, 2, 256, 512), F32),
            pltpu.VMEM((2, 256, 512), F32),
            pltpu.VMEM((3, 8, TILES_CH, CAP), jnp.int32),
            pltpu.VMEM(lists_shape, jnp.int16),
            pltpu.VMEM(lists_shape, jnp.int16),
            pltpu.VMEM((8, TAB_ROWS, 256), BF16),
        ] + [pltpu.VMEM((8, TILES_CH, CAP), jnp.int32)] * 4 + [pltpu.VMEM((8, TAB_ROWS, 256), BF16)] * 2 + [
            pltpu.VMEM((TILES_CH, 64, 64), F32),
            pltpu.VMEM((16, TILES_CH, 128), F32),
            pltpu.VMEM((16, TILES_CH, 128), F32),
            pltpu.VMEM((16, 128, 128), F32),
            pltpu.VMEM((4, 16, 16, 128), BF16),
            pltpu.VMEM((4, 16, 16, 128), BF16),
            pltpu.VMEM((3, 16, 16, 128), BF16),
            pltpu.VMEM((3, 16, 16, 128), BF16),
            pltpu.VMEM((16, 16, 128), F32),
            pltpu.VMEM((16, 16, 128), F32),
            pltpu.VMEM((3, 4, 16, 128), F32),
            pltpu.VMEM((3, 4, 16, 128), F32),
            pltpu.VMEM((8, 16, 128), F32),
            pltpu.VMEM((7, 16, 128), F32),
            dma((3,)), dma((2, 15)), dma((2, 15)), dma((8,)), dma((8,)), dma((2,)), dma((2,)), dma((8,)), dma((8,)),
            dma((3,)), dma((3,)), dma((3,)), dma((3,)),
            dma((3,)), dma((3,)), dma((3,)), dma((3,)),
            dma((7,)), dma((7,)),
        ],
        compiler_params=pltpu.CompilerParams(collective_id=0, has_side_effects=True),
        name="correlate_and_grid",
    )(voltages, tile_lists, offset_u, offset_v, kernels, owner_map)


def solution(mesh):
    placed = (
        P("chan", "stn", None),
        P("chan", None, None),
        P("chan", "stn", None, None),
        P("chan", "stn", None, None),
        P("chan", "stn", None, None),
        P("chan", None),
    )
    return jax.shard_map(
        on_device, mesh=mesh, in_specs=placed, out_specs=P(("chan", "stn"), None), check_vma=False
    )
```

```python
import math

import jax
import jax.numpy as jnp
from jax import lax
from jax.experimental import pallas as pl
from jax.experimental.pallas import tpu as pltpu
from jax.sharding import PartitionSpec as P

MESH = pl.DeviceIdType.MESH
TILE = 32
GRP = 32
SAMPLES = 1024
TILES_CH = 64
CAP = 128
GRID_TILES = 256
TAB_ROWS = 80
N_CHIPS = 8
F32 = jnp.float32
BF16 = jnp.bfloat16


def dot_nt(a, b):
    return lax.dot_general(a, b, (((1,), (1,)), ((), ())), preferred_element_type=F32)


def chan_kernel(volt, entries, off_u_in, off_v_in, kern, owner, out,
                xs, neg, gram, got, raw, packed, lists, tab, his, rows, offs_u, offs_v, found, sums,
                mine, theirs, dense, send_a, send_b, got_a, got_b, sum_a, sum_b, got_a2, got_b2, sum_z, got_z,
                raw_sem, v_send, v_recv, l_send, l_recv, own_sem, e_sem, t_send, t_recv,
                s_a, r_a, s_b, r_b, s_a2, r_a2, s_b2, r_b2, s_z, r_z):
    chan = lax.axis_index("chan")
    me = lax.axis_index("stn")
    chip = me // 2
    core = lax.rem(me, 2)
    z, xlo = chan // 2, lax.rem(chan, 2)
    xhi, y = me // 8, lax.rem(chip, 4)
    x = xhi * 2 + xlo

    def device(x_, y_, z_):
        return (z_ * 2 + lax.rem(x_, 2), (x_ // 2) * 8 + y_ * 2 + core)

    def slot_x(x_):
        return lax.rem(x_, 2) * 2 + x_ // 2

    def peer_x(d):
        return lax.rem(x + d, 4)

    def peer_y(d):
        return lax.rem(y + d, 4)

    def peer_z(d):
        return lax.rem(z + d, 8)

    partner = (chan, 2 * chip + 1 - core)
    peers = [(chan, lax.rem(me + j, 16)) for j in range(1, 16)]
    peers += [device(peer_x(d), y, z) for d in (1, 3)]
    peers += [device(x, y, peer_z(d)) for d in range(1, 8)]
    barrier = pltpu.get_barrier_semaphore()
    for peer in peers:
        pl.semaphore_signal(barrier, 1, device_id=peer, device_id_type=MESH)

    loads = [pltpu.make_async_copy(ref.at[:, 0], raw.at[n], raw_sem.at[n])
             for n, ref in enumerate((entries, off_u_in, off_v_in))]
    for copy in loads:
        copy.start()
    for copy in loads:
        copy.wait()

    def narrow(k, carry):
        for n in range(3):
            packed[k, n] = raw[n, k].astype(jnp.int16)
        return carry

    lax.fori_loop(0, N_CHIPS, narrow, 0)
    pl.semaphore_wait(barrier, len(peers))

    def send(src, dst, ss, rs, peer):
        copy = pltpu.make_async_remote_copy(src, dst, ss, rs, device_id=peer, device_id_type=MESH)
        copy.start()
        return copy

    list_core = me // 8
    list_slot = lax.rem(me, 8)

    def list_copy(k):
        return pltpu.make_async_remote_copy(
            packed.at[k], lists.at[list_slot], l_send.at[k], l_recv.at[list_slot],
            device_id=(chan, 2 * k + list_core), device_id_type=MESH)

    for k in range(N_CHIPS):
        @pl.when(2 * k + list_core != me)
        def _():
            list_copy(k).start()

        @pl.when(2 * k + list_core == me)
        def _():
            pltpu.make_async_copy(packed.at[k], lists.at[list_slot], l_recv.at[list_slot]).start()

    def volt_src(dest, half):
        return volt.at[dest // 2, :, pl.ds(pl.multiple_of(half * 2048 + lax.rem(dest, 2) * 1024, 1024), 1024)]

    def volt_dst(half):
        return xs.at[pl.ds(pl.multiple_of(me * GRP, GRP), GRP), pl.ds(half * 1024, 1024)]

    copies = []
    for half in range(2):
        for j in range(1, 16):
            dest = lax.rem(me + j, 16)
            copies.append(send(volt_src(dest, half), volt_dst(half), v_send.at[half, j - 1],
                               v_recv.at[half, j - 1], (chan, dest)))
    own = [pltpu.make_async_copy(volt_src(me, half), volt_dst(half), own_sem.at[half]) for half in range(2)]
    for copy in own:
        copy.start()

    for slot in range(8):
        pltpu.make_async_copy(packed.at[0], lists.at[slot], l_recv.at[slot]).wait()

    def prepare(g, carry):
        entry = lists[g, 0].astype(jnp.int32)
        shift = entry >> 10
        i = (entry >> 5) & 31
        j = entry & 31
        far = shift == 8
        his[g] = jnp.where(far, (i >> 3) * 32 + j, (shift & 7) * 32 + j)
        rows[g] = jnp.where(shift > 8, -1, jnp.where(far, 32 + (i & 7), i))
        offs_u[g] = lists[g, 1].astype(jnp.int32)
        offs_v[g] = lists[g, 2].astype(jnp.int32)
        return carry

    lax.fori_loop(0, 8, prepare, 0)
    iota = lambda shape, axis: lax.broadcasted_iota(jnp.int32, shape, axis)
    taps = kern[chip].astype(F32)
    ro, co = iota((64, 256), 0), iota((64, 256), 1)
    dist = jnp.where(ro // 32 == co // 128, co % 32 - ro % 32, -1)
    taps_v = jnp.zeros((64, 256), F32)
    for tap in range(8):
        taps_v = jnp.where(dist == tap, taps[1:2, tap:tap + 1], taps_v)
    taps_v = taps_v.astype(BF16)
    ro, co = iota((64, 64), 0), iota((64, 64), 1)
    dist = jnp.where(ro // 32 == co // 32, (ro % 8) * 4 + (ro % 32) // 8 - co % 32, -1)
    taps_u = jnp.zeros((64, 64), F32)
    for tap in range(8):
        taps_u = jnp.where(dist == tap, taps[0:1, tap:tap + 1], taps_u)
    taps_u = jnp.concatenate([taps_u, taps_u], axis=1).astype(BF16)
    ro = iota((128, 128), 0)
    low = ro % 64
    outer, inner, zq = low // 16, (low // 4) % 4, low % 4
    ys = jnp.where(ro < 64, outer, inner)
    xslot = jnp.where(ro < 64, inner, outer)
    cell = (zq + 4 * (ro // 64)) * 32 + xslot * 8 + ys * 2 + core
    owners = owner[pl.ds(chip, 1), :]
    owners = jnp.concatenate([owners, owners], axis=1)
    owner_hot = jnp.where(cell == owners, 1.0, 0.0).astype(BF16)

    for copy in own:
        copy.wait()
    for copy in copies:
        copy.wait()

    def products(block):
        row0 = pl.multiple_of(block * 256, 256)
        neg[:, :1024] = xs[pl.ds(row0, 256), 1024:]
        neg[:, 1024:] = -xs[pl.ds(row0, 256), :1024]
        for col in range(2):
            other = block if col == 0 else 1 - block
            right = xs[pl.ds(pl.multiple_of(other * 256, 256), 256), :]
            gram[block, 0, :, col * 256:(col + 1) * 256] = dot_nt(xs[pl.ds(row0, 256), :], right)
            gram[block, 1, :, col * 256:(col + 1) * 256] = dot_nt(neg[...], right)

    products(1 - core)
    exchange = send(gram.at[1 - core], got, e_sem.at[0], e_sem.at[1], partner)
    products(core)
    exchange.wait()

    lane, row = iota((GRP, 256), 1), iota((GRP, 256), 0)
    lane_grp8 = iota((8, 128), 1) // 32
    for g in range(8):
        fars = []
        for part in range(2):
            block = slice(g * GRP, (g + 1) * GRP)
            full = (gram[core, part, block, :] + got[part, block, :]) * (1.0 / 64.0)
            if g:
                full = pltpu.roll(full, 512 - g * GRP, 1)
            near = jnp.where(lane == row, 0.0, full[:, :256])
            tab[g, part * GRP:(part + 1) * GRP, :] = near.astype(BF16)
            far = jnp.zeros((8, 128), F32)
            for m in range(4):
                piece = full[m * 8:(m + 1) * 8, 256:384]
                if m:
                    piece = pltpu.roll(piece, m * 32, 1)
                far = jnp.where(lane_grp8 == m, piece, far)
            fars.append(jnp.where(core == 0, far, 0.0))
        far = jnp.concatenate(fars, axis=0)
        tab[g, 64:80, :] = jnp.concatenate([far, jnp.zeros((16, 128), F32)], axis=1).astype(BF16)

    ids16 = iota((16, 128), 0).astype(jnp.int16)
    hot_ids = [(iota((16, 128), 0) + 16 * n).astype(jnp.int16) for n in range(16)]
    far_ids = (iota((16, 128), 0) % 8 + 32).astype(jnp.int16)
    one, zero = jnp.ones((), BF16), jnp.zeros((), BF16)

    def line(ref, g, t):
        return jnp.broadcast_to(ref[g, pl.ds(t, 1), :], (16, 128)).astype(jnp.int16)

    def fetch(tp, g):
        hot = []
        for a in range(2):
            hi = line(his, g, 2 * tp + a)
            hot.append(jnp.concatenate([jnp.where(ids == hi, one, zero) for ids in hot_ids], axis=0))
        found[g, tp] = jnp.dot(tab[g], jnp.concatenate(hot, axis=1), preferred_element_type=F32).astype(BF16)

    def fetch_step(tp, carry):
        for g in range(8):
            fetch(tp, g)
        return carry

    lax.fori_loop(0, TILES_CH // 2, fetch_step, 0, unroll=4)

    def place(tp, g, left, right):
        picked = []
        for a in range(2):
            r = line(rows, g, 2 * tp + a)
            lanes = slice(a * 128, (a + 1) * 128)
            tiles = [found[g, tp, n * 16:(n + 1) * 16, lanes] for n in range(5)]
            here = [ids == r for ids in hot_ids[:2]]
            far = jnp.where(far_ids == r, tiles[4], zero).astype(F32)
            for part in range(2):
                value = zero
                for n in range(2):
                    value = jnp.where(here[n], tiles[part * 2 + n], value)
                value = value.astype(F32)
                value = value[:8] + value[8:] + far[part * 8:part * 8 + 8]
                for step in (4, 2, 1):
                    value = value + pltpu.roll(value, step, 0)
                picked.append(jnp.concatenate([value, value], axis=0).astype(BF16))
        for a in range(2):
            at_u = line(offs_u, g, 2 * tp + a)
            at_v = line(offs_v, g, 2 * tp + a)
            masks = [ids16 == at_v, hot_ids[1] == at_v]
            left[a].append(jnp.concatenate(
                [jnp.where(ids == at_u, one, zero) for ids in (ids16, hot_ids[1])], axis=0))
            right[a].append(jnp.concatenate(
                [jnp.where(masks[n % 2], picked[2 * a + n // 2], zero) for n in range(4)], axis=0))

    def place_step(tp, carry):
        left, right = [[], []], [[], []]
        for g in range(8):
            place(tp, g, left, right)
        for a in range(2):
            sums[2 * tp + a] = dot_nt(jnp.concatenate(left[a], axis=1), jnp.concatenate(right[a], axis=1))
        return carry

    lax.fori_loop(0, TILES_CH // 2, place_step, 0, unroll=4)

    lane_grp = iota((8, 128), 1) // 32

    def tile_copy(step):
        part = pl.ds(pl.multiple_of(step * 8, 8), 8)
        return pltpu.make_async_remote_copy(mine.at[:, part], theirs.at[:, part], t_send.at[step], t_recv.at[step],
                                            device_id=partner, device_id_type=MESH)

    def finish(step, carry):
        for b in range(4):
            t = step * 8 + b * 2
            value = sums[pl.ds(t, 2)].reshape(64, 64)
            high = value.astype(BF16)
            low_part = (value - high.astype(F32)).astype(BF16)
            spread = (jnp.dot(high, taps_v, preferred_element_type=F32)
                      + jnp.dot(low_part, taps_v, preferred_element_type=F32))
            high = spread.astype(BF16)
            low_part = (spread - high.astype(F32)).astype(BF16)
            cells = jnp.dot(taps_u, jnp.concatenate([high, low_part], axis=0), preferred_element_type=F32)
            for a in range(2):
                parts = []
                for part in range(2):
                    lanes = slice(part * 128, (part + 1) * 128)
                    tile = cells[a * 32:a * 32 + 8, lanes]
                    for ul in range(1, 4):
                        tile = jnp.where(lane_grp == ul, cells[a * 32 + ul * 8:a * 32 + ul * 8 + 8, lanes], tile)
                    parts.append(tile)
                mine.reshape(16 * TILES_CH, 128)[pl.ds(t + a, 16, stride=TILES_CH), :] = jnp.concatenate(parts, axis=0)
        tile_copy(step).start()
        return carry

    lax.fori_loop(0, TILES_CH // 8, finish, 0)
    for step in range(TILES_CH // 8):
        tile_copy(step).wait()

    for a in range(16):
        value = mine[a] + theirs[a]
        high = value.astype(BF16)
        low_part = (value - high.astype(F32)).astype(BF16)
        cells = jnp.dot(owner_hot, jnp.concatenate([high, low_part], axis=0), preferred_element_type=F32)
        dense[a] = cells
        for n in range(4):
            send_a[n, a] = cells[n * 16:(n + 1) * 16].astype(BF16)
            send_b[n, a] = cells[64 + n * 16:64 + (n + 1) * 16].astype(BF16)

    first = []
    for d in (2, 1, 3):
        first.append(send(send_a.at[peer_y(d)], got_a.at[d - 1], s_a.at[d - 1], r_a.at[d - 1],
                          device(x, peer_y(d), z)))
        first.append(send(send_b.at[slot_x(peer_x(d))], got_b.at[d - 1], s_b.at[d - 1], r_b.at[d - 1],
                          device(peer_x(d), y, z)))
    for copy in first:
        copy.wait()
    at_a = pl.ds(pl.multiple_of(y * 16, 16), 16)
    at_b = pl.ds(pl.multiple_of(64 + slot_x(x) * 16, 16), 16)
    for a in range(16):
        value = dense[a, at_a, :]
        for d in range(3):
            value = value + got_a[d, a].astype(F32)
        sum_a.reshape(256, 128)[pl.ds(a, 16, stride=16), :] = value
        value = dense[a, at_b, :]
        for d in range(3):
            value = value + got_b[d, a].astype(F32)
        sum_b.reshape(256, 128)[pl.ds(a, 16, stride=16), :] = value

    def four(slot):
        return pl.ds(pl.multiple_of(slot * 4, 4), 4)

    second = []
    for d in (2, 1, 3):
        second.append(send(sum_a.at[four(slot_x(peer_x(d)))], got_a2.at[d - 1], s_a2.at[d - 1], r_a2.at[d - 1],
                           device(peer_x(d), y, z)))
        second.append(send(sum_b.at[four(peer_y(d))], got_b2.at[d - 1], s_b2.at[d - 1], r_b2.at[d - 1],
                           device(x, peer_y(d), z)))
    for copy in second:
        copy.wait()
    sum_z[0:4] = sum_a[four(slot_x(x))] + got_a2[0] + got_a2[1] + got_a2[2]
    sum_z[4:8] = sum_b[four(y)] + got_b2[0] + got_b2[1] + got_b2[2]
    third = []
    for d in (4, 3, 5, 2, 6, 1, 7):
        third.append(send(sum_z.at[peer_z(d)], got_z.at[d - 1], s_z.at[d - 1], r_z.at[d - 1],
                          device(x, y, peer_z(d))))
    for k in range(N_CHIPS):
        @pl.when(2 * k + list_core != me)
        def _():
            list_copy(k).wait_send()
    for copy in third:
        copy.wait()
    value = sum_z[z]
    for d in range(7):
        value = value + got_z[d]
    for n in range(16):
        out[:, n * 128:(n + 1) * 128] = value[n:n + 1]


def on_device(voltages, kernels, tile_lists, offset_u, offset_v, owner_map):
    dma = pltpu.SemaphoreType.DMA
    anywhere, vmem = pl.BlockSpec(memory_space=pl.ANY), pl.BlockSpec(memory_space=pltpu.VMEM)
    lists_shape = (8, 3, TILES_CH, CAP)
    return pl.pallas_call(
        chan_kernel,
        out_shape=jax.ShapeDtypeStruct((1, 2048), F32),
        in_specs=[anywhere] * 4 + [vmem] * 2,
        out_specs=vmem,
        scratch_shapes=[
            pltpu.VMEM((512, 2048), BF16),
            pltpu.VMEM((256, 2048), BF16),
            pltpu.VMEM((2, 2, 256, 512), F32),
            pltpu.VMEM((2, 256, 512), F32),
            pltpu.VMEM((3, 8, TILES_CH, CAP), jnp.int32),
            pltpu.VMEM(lists_shape, jnp.int16),
            pltpu.VMEM(lists_shape, jnp.int16),
            pltpu.VMEM((8, TAB_ROWS, 256), BF16),
        ] + [pltpu.VMEM((8, TILES_CH, CAP), jnp.int32)] * 4 + [
            pltpu.VMEM((8, TILES_CH // 2, TAB_ROWS, 256), BF16),
            pltpu.VMEM((TILES_CH, 32, 64), F32),
            pltpu.VMEM((16, TILES_CH, 128), F32),
            pltpu.VMEM((16, TILES_CH, 128), F32),
            pltpu.VMEM((16, 128, 128), F32),
            pltpu.VMEM((4, 16, 16, 128), BF16),
            pltpu.VMEM((4, 16, 16, 128), BF16),
            pltpu.VMEM((3, 16, 16, 128), BF16),
            pltpu.VMEM((3, 16, 16, 128), BF16),
            pltpu.VMEM((16, 16, 128), F32),
            pltpu.VMEM((16, 16, 128), F32),
            pltpu.VMEM((3, 4, 16, 128), F32),
            pltpu.VMEM((3, 4, 16, 128), F32),
            pltpu.VMEM((8, 16, 128), F32),
            pltpu.VMEM((7, 16, 128), F32),
            dma((3,)), dma((2, 15)), dma((2, 15)), dma((8,)), dma((8,)), dma((2,)), dma((2,)), dma((8,)), dma((8,)),
            dma((3,)), dma((3,)), dma((3,)), dma((3,)),
            dma((3,)), dma((3,)), dma((3,)), dma((3,)),
            dma((7,)), dma((7,)),
        ],
        compiler_params=pltpu.CompilerParams(collective_id=0, has_side_effects=True),
        name="correlate_and_grid",
    )(voltages, tile_lists, offset_u, offset_v, kernels, owner_map)


def solution(mesh):
    placed = (
        P("chan", "stn", None),
        P("chan", None, None),
        P("chan", "stn", None, None),
        P("chan", "stn", None, None),
        P("chan", "stn", None, None),
        P("chan", None),
    )
    return jax.shard_map(
        on_device, mesh=mesh, in_specs=placed, out_specs=P(("chan", "stn"), None), check_vma=False
    )
```

```python
import math

import jax
import jax.numpy as jnp
from jax import lax
from jax.experimental import pallas as pl
from jax.experimental.pallas import tpu as pltpu
from jax.sharding import PartitionSpec as P

MESH = pl.DeviceIdType.MESH
TILE = 32
GRP = 32
SAMPLES = 1024
TILES_CH = 64
CAP = 128
GRID_TILES = 256
TAB_ROWS = 96
DEPTH = 192
N_CHIPS = 8
F32 = jnp.float32
BF16 = jnp.bfloat16


def dot_nt(a, b):
    return lax.dot_general(a, b, (((1,), (1,)), ((), ())), preferred_element_type=F32)


def chan_kernel(volt, entries, off_u_in, off_v_in, kern, owner, out,
                xs, neg, gram, got, raw, packed, lists, tab, his, rows, offs_u, offs_v, found, sums,
                mine, theirs, dense, send_a, send_b, got_a, got_b, sum_a, sum_b, got_a2, got_b2, sum_z, got_z,
                raw_sem, v_send, v_recv, l_send, l_recv, own_sem, e_sem, t_send, t_recv,
                s_a, r_a, s_b, r_b, s_a2, r_a2, s_b2, r_b2, s_z, r_z):
    chan = lax.axis_index("chan")
    me = lax.axis_index("stn")
    chip = me // 2
    core = lax.rem(me, 2)
    z, xlo = chan // 2, lax.rem(chan, 2)
    xhi, y = me // 8, lax.rem(chip, 4)
    x = xhi * 2 + xlo

    def device(x_, y_, z_):
        return (z_ * 2 + lax.rem(x_, 2), (x_ // 2) * 8 + y_ * 2 + core)

    def slot_x(x_):
        return lax.rem(x_, 2) * 2 + x_ // 2

    def peer_x(d):
        return lax.rem(x + d, 4)

    def peer_y(d):
        return lax.rem(y + d, 4)

    def peer_z(d):
        return lax.rem(z + d, 8)

    partner = (chan, 2 * chip + 1 - core)
    peers = [(chan, lax.rem(me + j, 16)) for j in range(1, 16)]
    peers += [device(peer_x(d), y, z) for d in (1, 3)]
    peers += [device(x, y, peer_z(d)) for d in range(1, 8)]
    loads = [pltpu.make_async_copy(ref.at[:, 0], raw.at[n], raw_sem.at[n])
             for n, ref in enumerate((entries, off_u_in, off_v_in))]
    for copy in loads:
        copy.start()
    barrier = pltpu.get_barrier_semaphore()
    for peer in peers:
        pl.semaphore_signal(barrier, 1, device_id=peer, device_id_type=MESH)

    pl.semaphore_wait(barrier, len(peers))

    def send(src, dst, ss, rs, peer):
        copy = pltpu.make_async_remote_copy(src, dst, ss, rs, device_id=peer, device_id_type=MESH)
        copy.start()
        return copy

    list_core = me // 8
    list_slot = lax.rem(me, 8)

    def list_copy(k):
        return pltpu.make_async_remote_copy(
            packed.at[k], lists.at[list_slot], l_send.at[k], l_recv.at[list_slot],
            device_id=(chan, 2 * k + list_core), device_id_type=MESH)

    def volt_src(dest, half):
        return volt.at[dest // 2, :, pl.ds(pl.multiple_of(half * 2048 + lax.rem(dest, 2) * 1024, 1024), 1024)]

    def volt_dst(half):
        return xs.at[pl.ds(pl.multiple_of(me * GRP, GRP), GRP), pl.ds(half * 1024, 1024)]

    copies = []
    for half in range(2):
        for j in range(1, 16):
            dest = lax.rem(me + j, 16)
            copies.append(send(volt_src(dest, half), volt_dst(half), v_send.at[half, j - 1],
                               v_recv.at[half, j - 1], (chan, dest)))
    own = [pltpu.make_async_copy(volt_src(me, half), volt_dst(half), own_sem.at[half]) for half in range(2)]
    for copy in own:
        copy.start()

    for copy in loads:
        copy.wait()

    def narrow(k, carry):
        for n in range(3):
            packed[k, n] = raw[n, k].astype(jnp.int16)
        return carry

    lax.fori_loop(0, N_CHIPS, narrow, 0)
    for k in range(N_CHIPS):
        @pl.when(2 * k + list_core != me)
        def _():
            list_copy(k).start()

        @pl.when(2 * k + list_core == me)
        def _():
            pltpu.make_async_copy(packed.at[k], lists.at[list_slot], l_recv.at[list_slot]).start()

    iota = lambda shape, axis: lax.broadcasted_iota(jnp.int32, shape, axis)
    taps = kern[chip].astype(F32)
    ro, co = iota((64, 256), 0), iota((64, 256), 1)
    dist = jnp.where(ro // 32 == co // 128, co % 32 - ro % 32, -1)
    taps_v = jnp.zeros((64, 256), F32)
    for tap in range(8):
        taps_v = jnp.where(dist == tap, taps[1:2, tap:tap + 1], taps_v)
    taps_v = taps_v.astype(BF16)
    ro, co = iota((64, 64), 0), iota((64, 64), 1)
    dist = jnp.where(ro // 32 == co // 32, (ro % 8) * 4 + (ro % 32) // 8 - co % 32, -1)
    taps_u = jnp.zeros((64, 64), F32)
    for tap in range(8):
        taps_u = jnp.where(dist == tap, taps[0:1, tap:tap + 1], taps_u)
    taps_u = jnp.concatenate([taps_u, taps_u], axis=1).astype(BF16)
    ro = iota((128, 128), 0)
    low = ro % 64
    outer, inner, zq = low // 16, (low // 4) % 4, low % 4
    ys = jnp.where(ro < 64, outer, inner)
    xslot = jnp.where(ro < 64, inner, outer)
    cell = (zq + 4 * (ro // 64)) * 32 + xslot * 8 + ys * 2 + core
    owners = owner[pl.ds(chip, 1), :]
    owners = jnp.concatenate([owners, owners], axis=1)
    owner_hot = jnp.where(cell == owners, 1.0, 0.0).astype(BF16)

    for copy in own:
        copy.wait()
    for copy in copies:
        copy.wait()

    def products(block):
        row0 = pl.multiple_of(block * 256, 256)
        neg[:, :1024] = xs[pl.ds(row0, 256), 1024:]
        neg[:, 1024:] = -xs[pl.ds(row0, 256), :1024]
        for col in range(2):
            other = block if col == 0 else 1 - block
            right = xs[pl.ds(pl.multiple_of(other * 256, 256), 256), :]
            gram[block, 0, :, col * 256:(col + 1) * 256] = dot_nt(xs[pl.ds(row0, 256), :], right)
            gram[block, 1, :, col * 256:(col + 1) * 256] = dot_nt(neg[...], right)

    products(1 - core)
    exchange = send(gram.at[1 - core], got, e_sem.at[0], e_sem.at[1], partner)
    products(core)
    exchange.wait()

    lane, row = iota((GRP, 512), 1), iota((GRP, 512), 0)
    masked = (lane == row) | ((lane >= 256) & (core == 1))
    low_lanes = iota((16, 256), 1) < 96
    for g in range(8):
        for part in range(2):
            block = slice(g * GRP, (g + 1) * GRP)
            full = (gram[core, part, block, :] + got[part, block, :]) * (1.0 / 64.0)
            if g:
                full = pltpu.roll(full, 512 - g * GRP, 1)
            full = jnp.where(masked, 0.0, full)
            tab[g, part * GRP:(part + 1) * GRP, :] = full[:, :256].astype(BF16)
            upper = pltpu.roll(full[:16], 512 - DEPTH, 1)[:, :256]
            lower = pltpu.roll(full[16:], 512 - DEPTH + 96, 1)[:, :256]
            tab[g, 64 + part * 16:80 + part * 16, :] = jnp.where(low_lanes, upper, lower).astype(BF16)

    for slot in range(8):
        pltpu.make_async_copy(packed.at[0], lists.at[slot], l_recv.at[slot]).wait()

    def prepare(g, carry):
        entry = lists[g, 0].astype(jnp.int32)
        shift = entry >> 10
        i = (entry >> 5) & 31
        j = entry & 31
        far = shift >= 6
        his[g] = jnp.where(far, (i >> 4) * 96 + (shift - 6) * 32 + j, shift * 32 + j)
        rows[g] = jnp.where(shift > 8, -1, jnp.where(far, 32 + (i & 15), i))
        offs_u[g] = lists[g, 1].astype(jnp.int32)
        offs_v[g] = lists[g, 2].astype(jnp.int32)
        return carry

    lax.fori_loop(0, 8, prepare, 0)
    ids16 = iota((16, 128), 0).astype(jnp.int16)
    hot_ids = [(iota((16, 128), 0) + 16 * n).astype(jnp.int16) for n in range(DEPTH // 16)]
    one, zero = jnp.ones((), BF16), jnp.zeros((), BF16)

    def line(ref, g, t):
        return jnp.broadcast_to(ref[g, pl.ds(t, 1), :], (16, 128)).astype(jnp.int16)

    def fetch(tp, g):
        hot = []
        for a in range(2):
            hi = line(his, g, 2 * tp + a)
            hot.append(jnp.concatenate([jnp.where(ids == hi, one, zero) for ids in hot_ids], axis=0))
        found[g, tp] = jnp.dot(tab[g, :, :DEPTH], jnp.concatenate(hot, axis=1), preferred_element_type=F32).astype(BF16)

    def fetch_step(tp, carry):
        for g in range(8):
            fetch(tp, g)
        return carry

    lax.fori_loop(0, TILES_CH // 2, fetch_step, 0, unroll=8)

    def place(tp, g, left, right):
        picked = []
        for a in range(2):
            r = line(rows, g, 2 * tp + a)
            lanes = slice(a * 128, (a + 1) * 128)
            tiles = [found[g, tp, n * 16:(n + 1) * 16, lanes] for n in range(6)]
            here = [ids == r for ids in hot_ids[:3]]
            for part in range(2):
                value = jnp.where(here[2], tiles[4 + part], zero)
                for n in range(2):
                    value = jnp.where(here[n], tiles[part * 2 + n], value)
                value = value.astype(F32)
                value = value[:8] + value[8:]
                for step in (4, 2, 1):
                    value = value + pltpu.roll(value, step, 0)
                picked.append(jnp.concatenate([value, value], axis=0).astype(BF16))
        for a in range(2):
            at_u = line(offs_u, g, 2 * tp + a)
            at_v = line(offs_v, g, 2 * tp + a)
            masks = [ids16 == at_v, hot_ids[1] == at_v]
            left[a].append(jnp.concatenate(
                [jnp.where(ids == at_u, one, zero) for ids in (ids16, hot_ids[1])], axis=0))
            right[a].append(jnp.concatenate(
                [jnp.where(masks[n % 2], picked[2 * a + n // 2], zero) for n in range(4)], axis=0))

    def place_pair(tp):
        left, right = [[], []], [[], []]
        for g in range(8):
            place(tp, g, left, right)
        for a in range(2):
            sums[2 * tp + a] = dot_nt(jnp.concatenate(left[a], axis=1), jnp.concatenate(right[a], axis=1))

    lane_grp = iota((8, 128), 1) // 32

    def tile_copy(step):
        part = pl.ds(pl.multiple_of(step * 8, 8), 8)
        return pltpu.make_async_remote_copy(mine.at[:, part], theirs.at[:, part], t_send.at[step], t_recv.at[step],
                                            device_id=partner, device_id_type=MESH)

    def spread_v(tp):
        value = sums[pl.ds(2 * tp, 2)].reshape(64, 64)
        high = value.astype(BF16)
        low_part = (value - high.astype(F32)).astype(BF16)
        return (jnp.dot(high, taps_v, preferred_element_type=F32)
                + jnp.dot(low_part, taps_v, preferred_element_type=F32))

    def spread_u(spread):
        high = spread.astype(BF16)
        low_part = (spread - high.astype(F32)).astype(BF16)
        return jnp.dot(taps_u, jnp.concatenate([high, low_part], axis=0), preferred_element_type=F32)

    def keep(tp, cells):
        for a in range(2):
            parts = []
            for part in range(2):
                lanes = slice(part * 128, (part + 1) * 128)
                tile = cells[a * 32:a * 32 + 8, lanes]
                for ul in range(1, 4):
                    tile = jnp.where(lane_grp == ul, cells[a * 32 + ul * 8:a * 32 + ul * 8 + 8, lanes], tile)
                parts.append(tile)
            mine.reshape(16 * TILES_CH, 128)[pl.ds(2 * tp + a, 16, stride=TILES_CH), :] = jnp.concatenate(parts, axis=0)

    def place_and_finish(step, carry):
        waiting = None
        for b in range(4):
            spread = spread_v(step * 4 - 4 + b)
            place_pair(step * 4 + b)
            if waiting is not None:
                keep(step * 4 - 5 + b, waiting)
            waiting = spread_u(spread)
        keep(step * 4 - 1, waiting)
        tile_copy(step - 1).start()
        return carry

    for b in range(4):
        place_pair(b)
    lax.fori_loop(1, TILES_CH // 8, place_and_finish, 0)
    last = [spread_v(TILES_CH // 2 - 4 + b) for b in range(4)]
    last = [spread_u(spread) for spread in last]
    for b in range(4):
        keep(TILES_CH // 2 - 4 + b, last[b])
    tile_copy(TILES_CH // 8 - 1).start()
    for step in range(TILES_CH // 8):
        tile_copy(step).wait()

    for a in range(16):
        value = mine[a] + theirs[a]
        high = value.astype(BF16)
        low_part = (value - high.astype(F32)).astype(BF16)
        cells = jnp.dot(owner_hot, jnp.concatenate([high, low_part], axis=0), preferred_element_type=F32)
        dense[a] = cells
        for n in range(4):
            send_a[n, a] = cells[n * 16:(n + 1) * 16].astype(BF16)
            send_b[n, a] = cells[64 + n * 16:64 + (n + 1) * 16].astype(BF16)

    first = []
    for d in (2, 1, 3):
        first.append(send(send_a.at[peer_y(d)], got_a.at[d - 1], s_a.at[d - 1], r_a.at[d - 1],
                          device(x, peer_y(d), z)))
        first.append(send(send_b.at[slot_x(peer_x(d))], got_b.at[d - 1], s_b.at[d - 1], r_b.at[d - 1],
                          device(peer_x(d), y, z)))
    for copy in first:
        copy.wait()
    at_a = pl.ds(pl.multiple_of(y * 16, 16), 16)
    at_b = pl.ds(pl.multiple_of(64 + slot_x(x) * 16, 16), 16)
    for a in range(16):
        value = dense[a, at_a, :]
        for d in range(3):
            value = value + got_a[d, a].astype(F32)
        sum_a.reshape(256, 128)[pl.ds(a, 16, stride=16), :] = value
        value = dense[a, at_b, :]
        for d in range(3):
            value = value + got_b[d, a].astype(F32)
        sum_b.reshape(256, 128)[pl.ds(a, 16, stride=16), :] = value

    def four(slot):
        return pl.ds(pl.multiple_of(slot * 4, 4), 4)

    second = []
    for d in (2, 1, 3):
        second.append(send(sum_a.at[four(slot_x(peer_x(d)))], got_a2.at[d - 1], s_a2.at[d - 1], r_a2.at[d - 1],
                           device(peer_x(d), y, z)))
        second.append(send(sum_b.at[four(peer_y(d))], got_b2.at[d - 1], s_b2.at[d - 1], r_b2.at[d - 1],
                           device(x, peer_y(d), z)))
    for copy in second:
        copy.wait()
    sum_z[0:4] = sum_a[four(slot_x(x))] + got_a2[0] + got_a2[1] + got_a2[2]
    sum_z[4:8] = sum_b[four(y)] + got_b2[0] + got_b2[1] + got_b2[2]
    third = []
    for d in (4, 3, 5, 2, 6, 1, 7):
        third.append(send(sum_z.at[peer_z(d)], got_z.at[d - 1], s_z.at[d - 1], r_z.at[d - 1],
                          device(x, y, peer_z(d))))
    for k in range(N_CHIPS):
        @pl.when(2 * k + list_core != me)
        def _():
            list_copy(k).wait_send()
    for copy in third:
        copy.wait()
    value = sum_z[z]
    for d in range(7):
        value = value + got_z[d]
    for n in range(16):
        out[:, n * 128:(n + 1) * 128] = value[n:n + 1]


def on_device(voltages, kernels, tile_lists, offset_u, offset_v, owner_map):
    dma = pltpu.SemaphoreType.DMA
    anywhere, vmem = pl.BlockSpec(memory_space=pl.ANY), pl.BlockSpec(memory_space=pltpu.VMEM)
    lists_shape = (8, 3, TILES_CH, CAP)
    return pl.pallas_call(
        chan_kernel,
        out_shape=jax.ShapeDtypeStruct((1, 2048), F32),
        in_specs=[anywhere] * 4 + [vmem] * 2,
        out_specs=vmem,
        scratch_shapes=[
            pltpu.VMEM((512, 2048), BF16),
            pltpu.VMEM((256, 2048), BF16),
            pltpu.VMEM((2, 2, 256, 512), F32),
            pltpu.VMEM((2, 256, 512), F32),
            pltpu.VMEM((3, 8, TILES_CH, CAP), jnp.int32),
            pltpu.VMEM(lists_shape, jnp.int16),
            pltpu.VMEM(lists_shape, jnp.int16),
            pltpu.VMEM((8, TAB_ROWS, 256), BF16),
        ] + [pltpu.VMEM((8, TILES_CH, CAP), jnp.int32)] * 4 + [
            pltpu.VMEM((8, TILES_CH // 2, TAB_ROWS, 256), BF16),
            pltpu.VMEM((TILES_CH, 32, 64), F32),
            pltpu.VMEM((16, TILES_CH, 128), F32),
            pltpu.VMEM((16, TILES_CH, 128), F32),
            pltpu.VMEM((16, 128, 128), F32),
            pltpu.VMEM((4, 16, 16, 128), BF16),
            pltpu.VMEM((4, 16, 16, 128), BF16),
            pltpu.VMEM((3, 16, 16, 128), BF16),
            pltpu.VMEM((3, 16, 16, 128), BF16),
            pltpu.VMEM((16, 16, 128), F32),
            pltpu.VMEM((16, 16, 128), F32),
            pltpu.VMEM((3, 4, 16, 128), F32),
            pltpu.VMEM((3, 4, 16, 128), F32),
            pltpu.VMEM((8, 16, 128), F32),
            pltpu.VMEM((7, 16, 128), F32),
            dma((3,)), dma((2, 15)), dma((2, 15)), dma((8,)), dma((8,)), dma((2,)), dma((2,)), dma((8,)), dma((8,)),
            dma((3,)), dma((3,)), dma((3,)), dma((3,)),
            dma((3,)), dma((3,)), dma((3,)), dma((3,)),
            dma((7,)), dma((7,)),
        ],
        compiler_params=pltpu.CompilerParams(collective_id=0, has_side_effects=True),
        name="correlate_and_grid",
    )(voltages, tile_lists, offset_u, offset_v, kernels, owner_map)


def solution(mesh):
    placed = (
        P("chan", "stn", None),
        P("chan", None, None),
        P("chan", "stn", None, None),
        P("chan", "stn", None, None),
        P("chan", "stn", None, None),
        P("chan", None),
    )
    return jax.shard_map(
        on_device, mesh=mesh, in_specs=placed, out_specs=P(("chan", "stn"), None), check_vma=False
    )
```

```python
import math

import jax
import jax.numpy as jnp
from jax import lax
from jax.experimental import pallas as pl
from jax.experimental.pallas import tpu as pltpu
from jax.sharding import PartitionSpec as P

MESH = pl.DeviceIdType.MESH
TILE = 32
GRP = 32
SAMPLES = 1024
TILES_CH = 64
CAP = 128
GRID_TILES = 256
TAB_ROWS = 96
DEPTH = 192
N_CHIPS = 8
F32 = jnp.float32
BF16 = jnp.bfloat16


def dot_nt(a, b):
    return lax.dot_general(a, b, (((1,), (1,)), ((), ())), preferred_element_type=F32)


def chan_kernel(volt, entries, off_u_in, off_v_in, kern_in, owner_in, out,
                kern, owner, xs, neg, gram, got, raw, packed, lists, tab, his, rows, offs_u, offs_v, found, sums,
                mine, theirs, dense, send_a, send_b, got_a, got_b, sum_a, sum_b, got_a2, got_b2, sum_z, got_z,
                raw_sem, v_send, v_recv, l_send, l_recv, own_sem, e_sem, t_send, t_recv,
                s_a, r_a, s_b, r_b, s_a2, r_a2, s_b2, r_b2, s_z, r_z):
    chan = lax.axis_index("chan")
    me = lax.axis_index("stn")
    chip = me // 2
    core = lax.rem(me, 2)
    z, xlo = chan // 2, lax.rem(chan, 2)
    xhi, y = me // 8, lax.rem(chip, 4)
    x = xhi * 2 + xlo

    def device(x_, y_, z_):
        return (z_ * 2 + lax.rem(x_, 2), (x_ // 2) * 8 + y_ * 2 + core)

    def slot_x(x_):
        return lax.rem(x_, 2) * 2 + x_ // 2

    def peer_x(d):
        return lax.rem(x + d, 4)

    def peer_y(d):
        return lax.rem(y + d, 4)

    def peer_z(d):
        return lax.rem(z + d, 8)

    partner = (chan, 2 * chip + 1 - core)
    peers = [device(x, y, peer_z(d)) for d in (4, 3, 5)]
    peers += [(chan, lax.rem(me + j, 16)) for j in (12, 13, 11, 10, 14, 4, 5, 3, 8, 9, 7, 6, 2, 15, 1)]
    peers += [device(x, y, peer_z(d)) for d in (2, 6, 1, 7)]
    peers += [device(peer_x(d), y, z) for d in (1, 3)]
    loads = [pltpu.make_async_copy(ref.at[:, 0], raw.at[n], raw_sem.at[n])
             for n, ref in enumerate((entries, off_u_in, off_v_in))]
    loads.append(pltpu.make_async_copy(kern_in, kern, raw_sem.at[3]))
    loads.append(pltpu.make_async_copy(owner_in, owner, raw_sem.at[4]))
    for copy in loads:
        copy.start()
    barrier = pltpu.get_barrier_semaphore()
    for peer in peers:
        pl.semaphore_signal(barrier, 1, device_id=peer, device_id_type=MESH)

    pl.semaphore_wait(barrier, len(peers))

    def send(src, dst, ss, rs, peer):
        copy = pltpu.make_async_remote_copy(src, dst, ss, rs, device_id=peer, device_id_type=MESH)
        copy.start()
        return copy

    list_core = me // 8
    list_slot = lax.rem(me, 8)

    def list_copy(k):
        return pltpu.make_async_remote_copy(
            packed.at[k], lists.at[list_slot], l_send.at[k], l_recv.at[list_slot],
            device_id=(chan, 2 * k + list_core), device_id_type=MESH)

    def volt_src(dest, half):
        return volt.at[dest // 2, :, pl.ds(pl.multiple_of(half * 2048 + lax.rem(dest, 2) * 1024, 1024), 1024)]

    def volt_dst(half):
        return xs.at[pl.ds(pl.multiple_of(me * GRP, GRP), GRP), pl.ds(half * 1024, 1024)]

    offsets = [(dx, dy, dc) for dx, dy in ((1, 2), (1, 1), (1, 3), (0, 2), (1, 0), (0, 1), (0, 3), (0, 0))
               for dc in (0, 1) if dx or dy or dc]
    copies = []
    for half in range(2):
        for n, (dx, dy, dc) in enumerate(offsets):
            dest = lax.rem(xhi + dx, 2) * 8 + peer_y(dy) * 2 + lax.rem(core + dc, 2)
            copies.append(send(volt_src(dest, half), volt_dst(half), v_send.at[half, n],
                               v_recv.at[half, n], (chan, dest)))
    own = [pltpu.make_async_copy(volt_src(me, half), volt_dst(half), own_sem.at[half]) for half in range(2)]
    for copy in own:
        copy.start()

    for copy in loads:
        copy.wait()

    def narrow(k, carry):
        for n in range(3):
            packed[k, n] = raw[n, k].astype(jnp.int16)
        return carry

    lax.fori_loop(0, N_CHIPS, narrow, 0)
    for k in range(N_CHIPS):
        @pl.when(2 * k + list_core != me)
        def _():
            list_copy(k).start()

        @pl.when(2 * k + list_core == me)
        def _():
            pltpu.make_async_copy(packed.at[k], lists.at[list_slot], l_recv.at[list_slot]).start()

    iota = lambda shape, axis: lax.broadcasted_iota(jnp.int32, shape, axis)
    taps = kern[chip].astype(F32)
    ro, co = iota((64, 256), 0), iota((64, 256), 1)
    dist = jnp.where(ro // 32 == co // 128, co % 32 - ro % 32, -1)
    taps_v = jnp.zeros((64, 256), F32)
    for tap in range(8):
        taps_v = jnp.where(dist == tap, taps[1:2, tap:tap + 1], taps_v)
    taps_v = taps_v.astype(BF16)
    ro, co = iota((64, 64), 0), iota((64, 64), 1)
    dist = jnp.where(ro // 32 == co // 32, (ro % 8) * 4 + (ro % 32) // 8 - co % 32, -1)
    taps_u = jnp.zeros((64, 64), F32)
    for tap in range(8):
        taps_u = jnp.where(dist == tap, taps[0:1, tap:tap + 1], taps_u)
    taps_u = jnp.concatenate([taps_u, taps_u], axis=1).astype(BF16)
    ro = iota((128, 128), 0)
    low = ro % 64
    outer, inner, zq = low // 16, (low // 4) % 4, low % 4
    ys = jnp.where(ro < 64, outer, inner)
    xslot = jnp.where(ro < 64, inner, outer)
    cell = (zq + 4 * (ro // 64)) * 32 + xslot * 8 + ys * 2 + core
    owners = owner[pl.ds(chip, 1), :]
    owners = jnp.concatenate([owners, owners], axis=1)
    owner_hot = jnp.where(cell == owners, 1.0, 0.0).astype(BF16)

    for copy in own:
        copy.wait()
    for copy in copies:
        copy.wait()

    def products(block):
        row0 = pl.multiple_of(block * 256, 256)
        neg[:, :1024] = xs[pl.ds(row0, 256), 1024:]
        neg[:, 1024:] = -xs[pl.ds(row0, 256), :1024]
        for col in range(2):
            other = block if col == 0 else 1 - block
            right = xs[pl.ds(pl.multiple_of(other * 256, 256), 256), :]
            gram[block, 0, :, col * 256:(col + 1) * 256] = dot_nt(xs[pl.ds(row0, 256), :], right)
            gram[block, 1, :, col * 256:(col + 1) * 256] = dot_nt(neg[...], right)

    products(1 - core)
    exchange = send(gram.at[1 - core], got, e_sem.at[0], e_sem.at[1], partner)
    products(core)
    exchange.wait()

    lane, row = iota((GRP, 512), 1), iota((GRP, 512), 0)
    masked = (lane == row) | ((lane >= 256) & (core == 1))
    low_lanes = iota((16, 256), 1) < 96
    for g in range(8):
        for part in range(2):
            block = slice(g * GRP, (g + 1) * GRP)
            full = (gram[core, part, block, :] + got[part, block, :]) * (1.0 / 64.0)
            if g:
                full = pltpu.roll(full, 512 - g * GRP, 1)
            full = jnp.where(masked, 0.0, full)
            tab[g, part * GRP:(part + 1) * GRP, :] = full[:, :256].astype(BF16)
            upper = pltpu.roll(full[:16], 512 - DEPTH, 1)[:, :256]
            lower = pltpu.roll(full[16:], 512 - DEPTH + 96, 1)[:, :256]
            tab[g, 64 + part * 16:80 + part * 16, :] = jnp.where(low_lanes, upper, lower).astype(BF16)

    for slot in range(8):
        pltpu.make_async_copy(packed.at[0], lists.at[slot], l_recv.at[slot]).wait()

    def prepare(g, carry):
        entry = lists[g, 0].astype(jnp.int32)
        shift = entry >> 10
        i = (entry >> 5) & 31
        j = entry & 31
        far = shift >= 6
        his[g] = jnp.where(far, (i >> 4) * 96 + (shift - 6) * 32 + j, shift * 32 + j)
        rows[g] = jnp.where(shift > 8, -1, jnp.where(far, 32 + (i & 15), i))
        offs_u[g] = lists[g, 1].astype(jnp.int32)
        offs_v[g] = lists[g, 2].astype(jnp.int32)
        return carry

    lax.fori_loop(0, 8, prepare, 0)
    ids16 = iota((16, 128), 0).astype(jnp.int16)
    hot_ids = [(iota((16, 128), 0) + 16 * n).astype(jnp.int16) for n in range(DEPTH // 16)]
    one, zero = jnp.ones((), BF16), jnp.zeros((), BF16)

    def line(ref, g, t):
        return jnp.broadcast_to(ref[g, pl.ds(t, 1), :], (16, 128)).astype(jnp.int16)

    def fetch(tp, g):
        hot = []
        for a in range(2):
            hi = line(his, g, 2 * tp + a)
            hot.append(jnp.concatenate([jnp.where(ids == hi, one, zero) for ids in hot_ids], axis=0))
        found[g, tp] = jnp.dot(tab[g, :, :DEPTH], jnp.concatenate(hot, axis=1), preferred_element_type=F32).astype(BF16)

    def fetch_step(tp, carry):
        for g in range(8):
            fetch(tp, g)
        return carry

    lax.fori_loop(0, TILES_CH // 2, fetch_step, 0, unroll=8)

    def place(tp, g, left, right):
        picked = []
        for a in range(2):
            r = line(rows, g, 2 * tp + a)
            lanes = slice(a * 128, (a + 1) * 128)
            tiles = [found[g, tp, n * 16:(n + 1) * 16, lanes] for n in range(6)]
            here = [ids == r for ids in hot_ids[:3]]
            for part in range(2):
                value = jnp.where(here[2], tiles[4 + part], zero)
                for n in range(2):
                    value = jnp.where(here[n], tiles[part * 2 + n], value)
                value = value.astype(F32)
                value = value[:8] + value[8:]
                for step in (4, 2, 1):
                    value = value + pltpu.roll(value, step, 0)
                picked.append(jnp.concatenate([value, value], axis=0).astype(BF16))
        for a in range(2):
            at_u = line(offs_u, g, 2 * tp + a)
            at_v = line(offs_v, g, 2 * tp + a)
            masks = [ids16 == at_v, hot_ids[1] == at_v]
            left[a].append(jnp.concatenate(
                [jnp.where(ids == at_u, one, zero) for ids in (ids16, hot_ids[1])], axis=0))
            right[a].append(jnp.concatenate(
                [jnp.where(masks[n % 2], picked[2 * a + n // 2], zero) for n in range(4)], axis=0))

    def place_pair(tp):
        left, right = [[], []], [[], []]
        for g in range(8):
            place(tp, g, left, right)
        for a in range(2):
            sums[2 * tp + a] = dot_nt(jnp.concatenate(left[a], axis=1), jnp.concatenate(right[a], axis=1))

    lane_grp = iota((8, 128), 1) // 32

    def tile_copy(step):
        part = pl.ds(pl.multiple_of(step * 8, 8), 8)
        return pltpu.make_async_remote_copy(mine.at[:, part], theirs.at[:, part], t_send.at[step], t_recv.at[step],
                                            device_id=partner, device_id_type=MESH)

    def spread_v(tp):
        value = sums[pl.ds(2 * tp, 2)].reshape(64, 64)
        high = value.astype(BF16)
        low_part = (value - high.astype(F32)).astype(BF16)
        return (jnp.dot(high, taps_v, preferred_element_type=F32)
                + jnp.dot(low_part, taps_v, preferred_element_type=F32))

    def spread_u(spread):
        high = spread.astype(BF16)
        low_part = (spread - high.astype(F32)).astype(BF16)
        return jnp.dot(taps_u, jnp.concatenate([high, low_part], axis=0), preferred_element_type=F32)

    def keep(tp, cells):
        for a in range(2):
            parts = []
            for part in range(2):
                lanes = slice(part * 128, (part + 1) * 128)
                tile = cells[a * 32:a * 32 + 8, lanes]
                for ul in range(1, 4):
                    tile = jnp.where(lane_grp == ul, cells[a * 32 + ul * 8:a * 32 + ul * 8 + 8, lanes], tile)
                parts.append(tile)
            mine.reshape(16 * TILES_CH, 128)[pl.ds(2 * tp + a, 16, stride=TILES_CH), :] = jnp.concatenate(parts, axis=0)

    def place_and_finish(step, carry):
        waiting = None
        for b in range(4):
            spread = spread_v(step * 4 - 4 + b)
            place_pair(step * 4 + b)
            if waiting is not None:
                keep(step * 4 - 5 + b, waiting)
            waiting = spread_u(spread)
        keep(step * 4 - 1, waiting)
        tile_copy(step - 1).start()
        return carry

    for b in range(4):
        place_pair(b)
    lax.fori_loop(1, TILES_CH // 8, place_and_finish, 0)
    last = [spread_v(TILES_CH // 2 - 4 + b) for b in range(4)]
    last = [spread_u(spread) for spread in last]
    for b in range(4):
        keep(TILES_CH // 2 - 4 + b, last[b])
    tile_copy(TILES_CH // 8 - 1).start()
    for step in range(TILES_CH // 8):
        tile_copy(step).wait()

    at_a = pl.ds(pl.multiple_of(y * 16, 16), 16)
    at_b = pl.ds(pl.multiple_of(64 + slot_x(x) * 16, 16), 16)

    def four(slot):
        return pl.ds(pl.multiple_of(slot * 4, 4), 4)

    first, second, third = [[], []], [[], []], [[], []]
    for h in range(2):
        part = pl.ds(h * 8, 8)
        for a in range(h * 8, h * 8 + 8):
            value = mine[a] + theirs[a]
            high = value.astype(BF16)
            low_part = (value - high.astype(F32)).astype(BF16)
            cells = jnp.dot(owner_hot, jnp.concatenate([high, low_part], axis=0), preferred_element_type=F32)
            dense[a] = cells
            for n in range(4):
                send_a[n, a] = cells[n * 16:(n + 1) * 16].astype(BF16)
                send_b[n, a] = cells[64 + n * 16:64 + (n + 1) * 16].astype(BF16)
        for d in (2, 1, 3):
            first[h].append(send(send_a.at[peer_y(d), part], got_a.at[d - 1, part], s_a.at[h, d - 1],
                                 r_a.at[h, d - 1], device(x, peer_y(d), z)))
            first[h].append(send(send_b.at[slot_x(peer_x(d)), part], got_b.at[d - 1, part], s_b.at[h, d - 1],
                                 r_b.at[h, d - 1], device(peer_x(d), y, z)))
    for h in range(2):
        part = pl.ds(h * 8, 8)
        for copy in first[h]:
            copy.wait()
        for a in range(h * 8, h * 8 + 8):
            value = dense[a, at_a, :]
            for d in range(3):
                value = value + got_a[d, a].astype(F32)
            sum_a.reshape(256, 128)[pl.ds(a, 16, stride=16), :] = value
            value = dense[a, at_b, :]
            for d in range(3):
                value = value + got_b[d, a].astype(F32)
            sum_b.reshape(256, 128)[pl.ds(a, 16, stride=16), :] = value
        for d in (2, 1, 3):
            second[h].append(send(sum_a.at[four(slot_x(peer_x(d))), part], got_a2.at[d - 1, :, part],
                                  s_a2.at[h, d - 1], r_a2.at[h, d - 1], device(peer_x(d), y, z)))
            second[h].append(send(sum_b.at[four(peer_y(d)), part], got_b2.at[d - 1, :, part],
                                  s_b2.at[h, d - 1], r_b2.at[h, d - 1], device(x, peer_y(d), z)))
    for h in range(2):
        part, rows8 = pl.ds(h * 8, 8), slice(h * 8, h * 8 + 8)
        for copy in second[h]:
            copy.wait()
        sum_z[0:4, rows8] = (sum_a[four(slot_x(x)), rows8] + got_a2[0, :, rows8] + got_a2[1, :, rows8]
                             + got_a2[2, :, rows8])
        sum_z[4:8, rows8] = sum_b[four(y), rows8] + got_b2[0, :, rows8] + got_b2[1, :, rows8] + got_b2[2, :, rows8]
        for d in (4, 3, 5, 2, 6, 1, 7):
            third[h].append(send(sum_z.at[peer_z(d), part], got_z.at[d - 1, part], s_z.at[h, d - 1],
                                 r_z.at[h, d - 1], device(x, y, peer_z(d))))
    for k in range(N_CHIPS):
        @pl.when(2 * k + list_core != me)
        def _():
            list_copy(k).wait_send()
    for copy in third[0] + third[1]:
        copy.wait()
    value = sum_z[z]
    for d in range(7):
        value = value + got_z[d]
    for n in range(16):
        out[:, n * 128:(n + 1) * 128] = value[n:n + 1]


def on_device(voltages, kernels, tile_lists, offset_u, offset_v, owner_map):
    dma = pltpu.SemaphoreType.DMA
    anywhere, vmem = pl.BlockSpec(memory_space=pl.ANY), pl.BlockSpec(memory_space=pltpu.VMEM)
    lists_shape = (8, 3, TILES_CH, CAP)
    return pl.pallas_call(
        chan_kernel,
        out_shape=jax.ShapeDtypeStruct((1, 2048), F32),
        in_specs=[anywhere] * 6,
        out_specs=vmem,
        scratch_shapes=[
            pltpu.VMEM(kernels.shape, BF16),
            pltpu.VMEM(owner_map.shape, jnp.int32),
            pltpu.VMEM((512, 2048), BF16),
            pltpu.VMEM((256, 2048), BF16),
            pltpu.VMEM((2, 2, 256, 512), F32),
            pltpu.VMEM((2, 256, 512), F32),
            pltpu.VMEM((3, 8, TILES_CH, CAP), jnp.int32),
            pltpu.VMEM(lists_shape, jnp.int16),
            pltpu.VMEM(lists_shape, jnp.int16),
            pltpu.VMEM((8, TAB_ROWS, 256), BF16),
        ] + [pltpu.VMEM((8, TILES_CH, CAP), jnp.int32)] * 4 + [
            pltpu.VMEM((8, TILES_CH // 2, TAB_ROWS, 256), BF16),
            pltpu.VMEM((TILES_CH, 32, 64), F32),
            pltpu.VMEM((16, TILES_CH, 128), F32),
            pltpu.VMEM((16, TILES_CH, 128), F32),
            pltpu.VMEM((16, 128, 128), F32),
            pltpu.VMEM((4, 16, 16, 128), BF16),
            pltpu.VMEM((4, 16, 16, 128), BF16),
            pltpu.VMEM((3, 16, 16, 128), BF16),
            pltpu.VMEM((3, 16, 16, 128), BF16),
            pltpu.VMEM((16, 16, 128), F32),
            pltpu.VMEM((16, 16, 128), F32),
            pltpu.VMEM((3, 4, 16, 128), F32),
            pltpu.VMEM((3, 4, 16, 128), F32),
            pltpu.VMEM((8, 16, 128), F32),
            pltpu.VMEM((7, 16, 128), F32),
            dma((5,)), dma((2, 15)), dma((2, 15)), dma((8,)), dma((8,)), dma((2,)), dma((2,)), dma((8,)), dma((8,)),
        ] + [dma((2, 3))] * 8 + [
            dma((2, 7)), dma((2, 7)),
        ],
        compiler_params=pltpu.CompilerParams(collective_id=0, has_side_effects=True),
        name="correlate_and_grid",
    )(voltages, tile_lists, offset_u, offset_v, kernels, owner_map)


def solution(mesh):
    placed = (
        P("chan", "stn", None),
        P("chan", None, None),
        P("chan", "stn", None, None),
        P("chan", "stn", None, None),
        P("chan", "stn", None, None),
        P("chan", None),
    )
    return jax.shard_map(
        on_device, mesh=mesh, in_specs=placed, out_specs=P(("chan", "stn"), None), check_vma=False
    )
```
